32 devices in a mesh: req: 4 (over y, core), seq: 4 (over z), tp: 2 (over x).
Axes of the slice: x: 2, y: 2, z: 4, core: 2. Of those that a mesh axis runs over, the one named last changes fastest.
Arguments:
- x_short: bfloat16 [32, 32, 1024], P(('req', 'seq')), may hold values from -6 to 6
- x_long: bfloat16 [4, 32, 1024], P('req'), may hold values from -6 to 6
- parents: int32 [32, 32], P(('req', 'seq')), may hold values from 0 to 30, as said below
- long_parents: int32 [4, 32], P('req'), may hold values from 0 to 30, as said below
- short_len: int32 [32], P(('req', 'seq')), may hold values from 1 to 512
- long_len: int32 [4], P('req'), may hold values from 1 to 1024
- doc_ids: int32 [32], replicated, may hold values from 0 to 31
- long_doc: int32 [4], replicated, may hold values from 0 to 31
- short_kv: bfloat16 [32, 2, 512, 1024], P(('req', 'seq'), None, None, 'tp'), as said below
- long_kv: bfloat16 [4, 2, 1024, 1024], P('req', None, 'seq', 'tp'), as said below
- enc_kv: bfloat16 [2, 32, 1024, 1024], P(None, None, ('req', 'seq'), 'tp'), as said below
- w_qkv: bfloat16 [3, 1024, 1024], P(None, None, 'tp'), may hold values from -0.1875 to 0.1875
- w_out: bfloat16 [1024, 1024], P('tp'), may hold values from -0.1875 to 0.1875
- w_cross_q: bfloat16 [1024, 1024], P(None, 'tp'), may hold values from -0.1875 to 0.1875
- w_cross_out: bfloat16 [1024, 1024], P('tp'), may hold values from -0.1875 to 0.1875
- w_up: bfloat16 [1024, 4096], P(None, 'tp'), may hold values from -0.1875 to 0.1875
- w_down: bfloat16 [4096, 1024], P('tp'), may hold values from -0.09375 to 0.09375
Outputs:
- y_short: bfloat16 [32, 32, 1024], P(('req', 'seq'))
- y_long: bfloat16 [4, 32, 1024], P('req')
The draws below stay inside these ranges and needn't reach their ends.
Inputs may be any that keep to these rules, and one draw needn't show every extreme that they name: parents[r, 0] is 0 and is ignored; for node i > 0, parents[r, i] lies in 0 to i - 1; the last node's parent is node 30. long_parents[r, 0] is 0 and is ignored; for node i > 0, long_parents[r, i] lies in 0 to i - 1; the last node's parent is node 30. `short_kv`: entries lie within -68 to 68. `long_kv`: entries lie within -68 to 68. `enc_kv`: entries lie within -68 to 68.
All inputs are finite; a program needn't handle non-finite values.
Results may differ from the reference program's by a relative error of at most 0.035.
Values may be sent and summed in bfloat16 or wider, within the bound.
No kernel may reach another device: no remote copies, remote signals or barrier semaphores. Data moves between devices by JAX's collectives and lax.ppermute only.
A program may use at most 192 MiB of HBM per device.

```python
import math
import jax
import jax.numpy as jnp
import numpy as np
from jax import lax

D = 1024
HEADS = 16
HD = 64
FF = 4096
DRAFT = 32
DOCS = 32
SHORT = 512
REQS = 32
LONG = 4
CACHE_L = 1024
ENC = 1024


def tree_parents(key, row_count):
    node_ids = jnp.arange(DRAFT, dtype=jnp.int32)
    upper = jnp.maximum(node_ids, 1)
    drawn = jax.random.randint(key, (row_count, DRAFT), 0, upper).astype(jnp.int32)
    return drawn.at[:, DRAFT - 1].set(DRAFT - 2).astype(jnp.int32)


def draw_parents(key, part):
    return tree_parents(jax.random.fold_in(key, 11), REQS)


def draw_long_parents(key, part):
    return tree_parents(jax.random.fold_in(key, 12), LONG)


def ragged(key, item_count, longest):
    key_one, key_two = jax.random.split(key)
    lengths = jax.random.randint(key_one, (item_count,), 1, longest + 1)
    shorter = jax.random.randint(key_two, (item_count,), 0, 2)
    lengths = jnp.where(shorter == 1, (lengths + 7) // 8, lengths)
    return lengths.at[0].set(longest).astype(jnp.int32)


def draw_short_len(key, part):
    return ragged(jax.random.fold_in(key, 21), REQS, SHORT)


def draw_long_len(key, part):
    return ragged(jax.random.fold_in(key, 22), LONG, CACHE_L)


def spiked_draw(key, shape):
    key_one = jax.random.fold_in(key, 0)
    values = jnp.clip(jax.random.normal(key_one, shape, jnp.float32), -6.0, 6.0)
    return values.astype(jnp.bfloat16)


def draw_short_kv(key, part):
    return spiked_draw(jax.random.fold_in(key, 33), (REQS, 2, SHORT, D))


def draw_long_kv(key, part):
    return spiked_draw(jax.random.fold_in(key, 31), (LONG, 2, CACHE_L, D))


def draw_enc_kv(key, part):
    return spiked_draw(jax.random.fold_in(key, 32), (2, DOCS, ENC, D))


def touch_ends(values, rng, smallest, high):
    dims = values.shape
    spot = [jax.random.randint(jax.random.fold_in(rng, axis), (), 0, dims[axis]) for axis in range(len(dims))]
    values = values.at[tuple(spot)].set(smallest)
    longest = dims.index(max(dims))
    spot[longest] = (spot[longest] + 1) % dims[longest]
    return values.at[tuple(spot)].set(high)


def block_levels(key, extent, pieces, low, high):
    def one(dim, parts):
        steps = jax.random.uniform(jax.random.fold_in(jax.random.fold_in(key, 6), dim), (parts,), jnp.float32, low / len(pieces), high / len(pieces))
        return jnp.repeat(jnp.exp(steps), extent[dim] // parts).reshape((-1,) + (1,) * (len(extent) - dim - 1))

    factor_of = one(*pieces[0])
    for cut in pieces[1:]:
        factor_of = factor_of * one(*cut)
    return factor_of


def cumulative_ranks(number_of, skew):
    portions = [(1 << 20) // math.isqrt(grade ** skew) + 1 for grade in range(1, number_of + 1)]
    scale = 1 + sum(portions) // (1 << 30)
    return np.cumsum(np.array([max(1, weight // scale) for weight in portions]))


def skewed_ids(rng, shape, amount, slope):
    listing = cumulative_ranks(amount, slope)
    pick = jax.random.randint(jax.random.fold_in(rng, 1), shape, 0, int(listing[amount - 1]))
    rank = jnp.searchsorted(jnp.asarray(listing, jnp.int32), pick, side="right")
    return jax.random.permutation(jax.random.fold_in(rng, 2), amount)[rank].astype(jnp.int32)


def bell_draw(key, extent, deviation, reach, cuts=(), held_as=jnp.bfloat16):
    entries = deviation * jax.random.normal(key, extent, jnp.float32)
    if cuts:
        entries = entries * block_levels(key, extent, cuts, -0.22, 0.18)
    return jnp.clip(entries, -reach, reach).astype(held_as)


def setup_inputs(seed: int = 0) -> dict:
    splits = jax.random.split(jax.random.key(seed), 18)
    return {
        "x_short": bell_draw(splits[0], (REQS, DRAFT, D), 1.0, 6.0, ((0, 16),)),
        "x_long": bell_draw(splits[1], (LONG, DRAFT, D), 1.0, 6.0, ((0, 4),)),
        "parents": draw_parents(jax.random.fold_in(splits[17], 71), 0),
        "long_parents": draw_long_parents(jax.random.fold_in(splits[17], 71), 0),
        "short_len": draw_short_len(jax.random.fold_in(splits[17], 71), 0),
        "long_len": draw_long_len(jax.random.fold_in(splits[17], 71), 0),
        "doc_ids": touch_ends(skewed_ids(splits[6], (REQS,), DOCS, 2), jax.random.fold_in(splits[6], 3), 0, DOCS - 1).astype(jnp.int32),
        "long_doc": touch_ends(jax.random.randint(splits[7], (LONG,), 0, DOCS), jax.random.fold_in(splits[7], 1), 0, DOCS - 1).astype(jnp.int32),
        "short_kv": draw_short_kv(jax.random.fold_in(splits[17], 71), 0),
        "long_kv": draw_long_kv(jax.random.fold_in(splits[17], 71), 0),
        "enc_kv": draw_enc_kv(jax.random.fold_in(splits[17], 71), 0),
        "w_qkv": bell_draw(splits[11], (3, D, D), D ** -0.5, 0.1875, ((2, 2),)),
        "w_out": bell_draw(splits[12], (D, D), D ** -0.5, 0.1875, ((0, 2),)),
        "w_cross_q": bell_draw(splits[13], (D, D), D ** -0.5, 0.1875, ((1, 2),)),
        "w_cross_out": bell_draw(splits[14], (D, D), D ** -0.5, 0.1875, ((0, 2),)),
        "w_up": bell_draw(splits[15], (D, FF), D ** -0.5, 0.1875, ((1, 2),)),
        "w_down": bell_draw(splits[16], (FF, D), FF ** -0.5, 0.09375, ((0, 2),)),
    }


MASKED_SCORE = -1e+30
NORM_EPSILON = 1e-05
PRECISE = lax.Precision.HIGHEST

def ancestry(parents):
    node_ids = jnp.arange(parents.shape[-1], dtype=jnp.int32)
    parent_hot = (parents[..., :, None] == node_ids[None, None, :]).astype(jnp.float32)
    parent_hot = parent_hot * (node_ids[:, None] > 0).astype(jnp.float32)
    closure = jnp.eye(parents.shape[-1], dtype=jnp.float32)[None] + parent_hot
    path_span = 1
    while path_span < parents.shape[-1]:
        closure = jnp.minimum(jnp.einsum('rij,rjk->rik', closure, closure, precision=PRECISE), 1.0)
        path_span = path_span * 2
    return closure > 0.5

def partial_softmax(queries, key_rows, value_rows, allowed):
    scores = jnp.einsum('nhe,che->hnc', queries.astype(jnp.float32), key_rows.astype(jnp.float32), precision=PRECISE) * HD ** (-0.5)
    scores = jnp.where(allowed, scores, MASKED_SCORE)
    maxima = lax.optimization_barrier(jnp.max(scores, axis=-1))
    weights = jnp.where(allowed, jnp.exp(scores - maxima[..., None]), 0.0)
    totals = lax.optimization_barrier(jnp.sum(weights, axis=-1))
    weighted = jnp.einsum('hnc,che->hne', weights, value_rows.astype(jnp.float32), precision=PRECISE)
    return (maxima, totals, weighted)

def combine(state_one, state_two):
    joint_max = jnp.maximum(state_one[0], state_two[0])
    scale_one = jnp.exp(state_one[0] - joint_max)
    scale_two = jnp.exp(state_two[0] - joint_max)
    return (joint_max, state_one[1] * scale_one + state_two[1] * scale_two, state_one[2] * scale_one[..., None] + state_two[2] * scale_two[..., None])

def finish(partial_state):
    result = partial_state[2] / partial_state[1][..., None]
    return jnp.transpose(result, (1, 0, 2)).reshape(result.shape[1], -1).astype(jnp.bfloat16)

def normalize(row_values):
    centered = row_values - lax.optimization_barrier(jnp.mean(row_values, axis=-1, keepdims=True))
    return centered * lax.rsqrt(lax.optimization_barrier(jnp.mean(centered * centered, axis=-1, keepdims=True)) + NORM_EPSILON)

def self_attend(items):
    query_rows, key_rows, value_rows, cache_kv, length, tree_mask = items
    cache_span = cache_kv.shape[1]
    cache_keys = cache_kv[0].reshape(cache_span, HEADS, HD)
    cache_values = cache_kv[1].reshape(cache_span, HEADS, HD)
    valid_keys = jnp.arange(cache_span, dtype=jnp.int32) < length
    cache_part = partial_softmax(query_rows, cache_keys, cache_values, valid_keys[None, None, :])
    draft_part = partial_softmax(query_rows, key_rows, value_rows, tree_mask[None])
    return finish(combine(cache_part, draft_part))

def reference(x_short, x_long, parents, long_parents, short_len, long_len, doc_ids, long_doc, short_kv, long_kv, enc_kv, w_qkv, w_out, w_cross_q, w_cross_out, w_up, w_down):
    inputs = jnp.concatenate([x_short, x_long], 0)
    total_req = inputs.shape[0]
    flat_rows = inputs.reshape(-1, D)
    projected = [jnp.dot(flat_rows, w_qkv[member], preferred_element_type=jnp.float32).astype(jnp.bfloat16).reshape(total_req, DRAFT, HEADS, HD) for member in range(3)]
    queries, key_rows, value_rows = projected
    short_out = lax.map(self_attend, (queries[:REQS], key_rows[:REQS], value_rows[:REQS], short_kv, short_len, ancestry(parents)))
    long_out = lax.map(self_attend, (queries[REQS:], key_rows[REQS:], value_rows[REQS:], long_kv, long_len, ancestry(long_parents)))
    attn = jnp.concatenate([short_out, long_out], 0).reshape(-1, D)
    attn_sum = jnp.dot(attn, w_out, preferred_element_type=jnp.float32)
    hidden_one = normalize(flat_rows.astype(jnp.float32) + attn_sum).astype(jnp.bfloat16)
    cross_queries = jnp.dot(hidden_one, w_cross_q, preferred_element_type=jnp.float32).astype(jnp.bfloat16).reshape(total_req, DRAFT, HEADS, HD)
    documents = jnp.concatenate([doc_ids, long_doc], 0)

    def cross_one(items):
        query_rows, document = items
        enc_keys = enc_kv[0][document].reshape(ENC, HEADS, HD)
        enc_values = enc_kv[1][document].reshape(ENC, HEADS, HD)
        allowed = jnp.ones((1, 1, ENC), dtype=bool)
        return finish(partial_softmax(query_rows, enc_keys, enc_values, allowed))
    cross = lax.map(cross_one, (cross_queries, documents)).reshape(-1, D)
    cross_sum = jnp.dot(cross, w_cross_out, preferred_element_type=jnp.float32)
    hidden_two = normalize(hidden_one.astype(jnp.float32) + cross_sum).astype(jnp.bfloat16)
    upward = jnp.dot(hidden_two, w_up, preferred_element_type=jnp.float32)
    activated = jax.nn.gelu(upward, approximate=False).astype(jnp.bfloat16)
    downward = jnp.dot(activated, w_down, preferred_element_type=jnp.float32)
    final_rows = normalize(hidden_two.astype(jnp.float32) + downward).astype(jnp.bfloat16)
    y_short = final_rows[:REQS * DRAFT].reshape(REQS, DRAFT, D)
    y_long = final_rows[REQS * DRAFT:].reshape(LONG, DRAFT, D)
    return (y_short, y_long)
```

```python
import functools

import jax
import jax.numpy as jnp
from jax import lax
from jax.experimental import pallas as pl
from jax.experimental.pallas import tpu as pltpu
from jax.sharding import PartitionSpec as P

HD = 64
LANES = 128
CORES = 2
PIECES = 3
MASKED = -1e30
EPS = 1e-05
F32 = jnp.float32
BF16 = jnp.bfloat16
VMEM = pl.BlockSpec(memory_space=pltpu.VMEM)
SMEM = pl.BlockSpec(memory_space=pltpu.SMEM)
ANY = pl.BlockSpec(memory_space=pl.ANY)


def iota(shape, axis):
    return lax.broadcasted_iota(jnp.int32, shape, axis)


def dot(a, b):
    return lax.dot_general(a, b, (((1,), (0,)), ((), ())), preferred_element_type=F32)


def dot_t(a, b):
    return lax.dot_general(a, b, (((1,), (1,)), ((), ())), preferred_element_type=F32)


def normalize(v):
    centered = v - jnp.mean(v, axis=-1, keepdims=True)
    return centered * lax.rsqrt(jnp.mean(centered * centered, axis=-1, keepdims=True) + EPS)


def head_mask(heads, rows, width):
    shape = (heads * rows, width)
    return (iota(shape, 0) // rows == iota(shape, 1) // HD).astype(F32)


def spread_heads(q, heads, mask):
    return jnp.concatenate([q] * heads, axis=0) * mask.astype(BF16)


def weigh(p, v):
    high = p.astype(BF16)
    return dot(high, v)


def fold_heads(o, heads):
    return jnp.sum(o.reshape(heads, o.shape[0] // heads, o.shape[1]), axis=0)


def pieces_of(x):
    high = x.astype(BF16)
    rest = x - high.astype(F32)
    mid = rest.astype(BF16)
    low = (rest - mid.astype(F32)).astype(BF16)
    return high, mid, low


def stat_block(lse, heads, rows):
    shape = (heads * rows, LANES)
    lane = iota(shape, 1)
    high, mid, low = (m.astype(F32) for m in pieces_of(lse))
    value = jnp.where(lane < heads, high, jnp.where(lane < 2 * heads, mid, low))
    keep = jnp.logical_and(lane % heads == iota(shape, 0) // rows, lane < PIECES * heads)
    return fold_heads(jnp.where(keep, value, 0.0), heads).astype(BF16)


def expand_stats(stats, heads):
    width = heads * HD
    lane = iota((LANES, width), 0)
    hot = jnp.logical_and(lane % heads == iota((LANES, width), 1) // HD, lane < PIECES * heads)
    return dot(stats, hot.astype(F32).astype(BF16))


def partial_payload(qs, k, v, allowed, mask, heads, rows):
    s = dot_t(qs, k) * HD ** (-0.5)
    if allowed is not None:
        s = jnp.where(allowed, s, MASKED)
    m = jnp.max(s, axis=-1, keepdims=True)
    p = jnp.exp(s - m)
    if allowed is not None:
        p = jnp.where(allowed, p, 0.0)
    l = jnp.maximum(jnp.sum(p, axis=-1, keepdims=True), 1e-30)
    o = fold_heads(weigh(p, v) * (mask / l), heads)
    return o.astype(BF16), stat_block(m + jnp.log(l), heads, rows)


def qkv_kernel(len_ref, xs_ref, xl_ref, w_ref, kv_ref, qkv_ref, pay_ref):
    short_rows = xs_ref.shape[0] * xs_ref.shape[1]
    rows, model = xl_ref.shape[1:]
    width = w_ref.shape[2]
    heads = width // HD
    x = jnp.concatenate([xs_ref[...].reshape(short_rows, model), xl_ref[0]], axis=0)
    for member in range(3):
        qkv_ref[member] = dot(x, w_ref[member]).astype(BF16)
    mask = head_mask(heads, rows, width)
    qs = spread_heads(qkv_ref[0, short_rows:, :], heads, mask)
    span = kv_ref.shape[2]
    positions = iota((1, span), 1) + lax.axis_index("seq") * span
    o, stats = partial_payload(
        qs, kv_ref[0, 0], kv_ref[0, 1], positions < len_ref[0], mask, heads, rows
    )
    pay_ref[:, :width] = o
    pay_ref[:, width:] = stats


def attend_kernel(hops, len_ref, ps_ref, pl_ref, qkv_ref, skv_ref, wo_ref, *rest):
    pay_refs, (out_ref, attn, pays) = rest[: hops + 1], rest[hops + 1 :]
    requests, _, span, width = skv_ref.shape
    heads = width // HD
    rows = ps_ref.shape[1]
    zed = lax.axis_index("seq")
    seqs = hops + 1
    for hop in range(seqs):
        pays[lax.rem(zed - hop + seqs, seqs)] = pay_refs[hop][...]
    mask = head_mask(heads, rows, width)
    node_j = iota((rows, rows), 0)
    node_i = iota((rows, rows), 1)
    eye = (node_i == node_j).astype(F32)

    def tree(parents):
        hot = jnp.logical_and(parents == node_j, node_i > 0).astype(F32)
        closure = eye + hot
        reach = 1
        while reach < rows:
            b = closure.astype(BF16)
            closure = jnp.minimum(dot(b, b), 1.0)
            reach *= 2
        flat = lax.dot_general(
            closure.astype(BF16),
            eye.astype(BF16),
            (((0,), (0,)), ((), ())),
            preferred_element_type=F32,
        )
        return jnp.concatenate([flat] * heads, axis=0) > 0.5

    for j in range(requests):
        row = j * rows
        qs = spread_heads(qkv_ref[0, row : row + rows, :], heads, mask)
        allowed = iota((1, span), 1) < len_ref[j]
        s = jnp.where(allowed, dot_t(qs, skv_ref[j, 0]) * HD ** (-0.5), MASKED)
        allowed_d = tree(ps_ref[j : j + 1, :])
        d = jnp.where(
            allowed_d, dot_t(qs, qkv_ref[1, row : row + rows, :]) * HD ** (-0.5), MASKED
        )
        m = jnp.maximum(jnp.max(s, axis=-1, keepdims=True), jnp.max(d, axis=-1, keepdims=True))
        p = jnp.where(allowed, jnp.exp(s - m), 0.0)
        pd = jnp.where(allowed_d, jnp.exp(d - m), 0.0)
        l = jnp.sum(p, axis=-1, keepdims=True) + jnp.sum(pd, axis=-1, keepdims=True)
        o = weigh(p, skv_ref[j, 1]) + weigh(pd, qkv_ref[2, row : row + rows, :])
        attn[row : row + rows, :] = fold_heads(o * (mask / l), heads).astype(BF16)

    row = requests * rows
    qs = spread_heads(qkv_ref[0, row:, :], heads, mask)
    o, stats = partial_payload(
        qs, qkv_ref[1, row:, :], qkv_ref[2, row:, :], tree(pl_ref[...]), mask, heads, rows
    )
    values = [o.astype(F32)] + [pays[z, :, :width].astype(F32) for z in range(seqs)]
    scores = [expand_stats(stats, heads)] + [
        expand_stats(pays[z, :, width:], heads) for z in range(seqs)
    ]
    attn[row:, :] = merge(values, scores).astype(BF16)
    out_ref[...] = dot(attn[...], wo_ref[...]).astype(BF16)


def merge(values, scores):
    top = functools.reduce(jnp.maximum, scores)
    total = None
    for value, score in zip(values, scores):
        w = jnp.exp(score - top)
        total = w if total is None else total + w
        acc = w * value if total is w else acc + w * value
    return acc / total


def query_kernel(xs_ref, xl_ref, a_ref, b_ref, w_ref, h_ref, q_ref, qs_ref):
    short_rows = xs_ref.shape[0] * xs_ref.shape[1]
    x = jnp.concatenate([xs_ref[...].reshape(short_rows, -1), xl_ref[0]], axis=0).astype(F32)
    h = normalize(x + (a_ref[...].astype(F32) + b_ref[...].astype(F32))).astype(BF16)
    h_ref[...] = h
    q = dot(h, w_ref[...]).astype(BF16)
    q_ref[...] = q[short_rows:]
    qs_ref[...] = q[:short_rows]


def cross_kernel(
    seqs, requests, group_ref, doc_ref, long_ref, own_ref, other_ref, q_ref, pay_ref, kv, sems
):
    pay_rows = pay_ref.shape[1]
    width = q_ref.shape[1]
    heads = width // HD
    span = own_ref.shape[2]
    short_total = seqs * requests
    rows = q_ref.shape[0] // (short_total + 1)
    group = group_ref[0]
    zed = lax.axis_index("seq")

    def doc_of(e):
        place = lax.rem(zed - e // requests + seqs, seqs)
        at = (group * seqs + place) * requests + lax.rem(e, requests)
        return doc_ref[at]

    def copies(e, doc):
        return (
            pltpu.make_async_copy(own_ref.at[:, doc], kv.at[e, :, pl.ds(0, span)], sems.at[e, 0]),
            pltpu.make_async_copy(
                other_ref.at[:, doc], kv.at[e, :, pl.ds(span, span)], sems.at[e, 1]
            ),
        )

    def start(e, carry):
        for copy in copies(e, doc_of(e)):
            copy.start()
        return carry

    for copy in copies(short_total, long_ref[group]):
        copy.start()
    lax.fori_loop(0, short_total, start, 0)
    mask = head_mask(heads, rows, width)

    def one(e, doc):
        for copy in copies(e, doc):
            copy.wait()
        qs = spread_heads(q_ref[pl.ds(pl.multiple_of(e * rows, rows), rows), :], heads, mask)
        return partial_payload(qs, kv[e, 0], kv[e, 1], None, mask, heads, rows)

    o, stats = one(short_total, long_ref[group])
    for k in range(seqs):
        pay_ref[k, requests * rows :, :width] = o
        pay_ref[k, requests * rows :, width:] = stats
    for e in range(short_total):
        o, stats = one(e, doc_of(e))
        k, row = e // requests, (e % requests) * rows
        pay_ref[k, row : row + rows, :width] = o
        pay_ref[k, row : row + rows, width:] = stats


def merge_kernel(places, seqs, w_ref, *rest):
    ins, (out_ref, pays, cross) = rest[: len(places)], rest[len(places) :]
    rows, width = cross.shape
    heads = width // HD
    pairs = lax.axis_size("req") // CORES
    yed = lax.axis_index("req") // CORES
    zed = lax.axis_index("seq")
    for ref, (dy, dz) in zip(ins, places):
        at = lax.rem(yed - dy + pairs, pairs) * seqs + lax.rem(zed + dz, seqs)
        pays[at] = ref[...]
    step = 32
    for row in range(0, rows, step):
        part = slice(row, row + step)
        values = [pays[s, part, :width].astype(F32) for s in range(len(places))]
        scores = [expand_stats(pays[s, part, width:], heads) for s in range(len(places))]
        cross[part, :] = merge(values, scores).astype(BF16)
    out_ref[...] = dot(cross[...], w_ref[...]).astype(BF16)


def gelu(x):
    return 0.5 * x * (1.0 + lax.erf(x * 0.5**0.5))


def ffn_kernel(h_ref, a_ref, b_ref, up_ref, down_ref, h2_ref, out_ref, acc):
    step = pl.program_id(0)

    @pl.when(step == 0)
    def _():
        total = h_ref[...].astype(F32) + (a_ref[...].astype(F32) + b_ref[...].astype(F32))
        h2_ref[...] = normalize(total).astype(BF16)

    act = gelu(dot(h2_ref[...], up_ref[...])).astype(BF16)
    part = dot(act, down_ref[...])

    @pl.when(step == 0)
    def _():
        acc[...] = part

    @pl.when(step > 0)
    def _():
        acc[...] += part

    @pl.when(step == pl.num_programs(0) - 1)
    def _():
        out_ref[...] = acc[...].astype(BF16)


def final_kernel(h_ref, a_ref, b_ref, ys_ref, yl_ref):
    total = h_ref[...].astype(F32) + (a_ref[...].astype(F32) + b_ref[...].astype(F32))
    y = normalize(total).astype(BF16)
    short_rows = ys_ref.shape[0] * ys_ref.shape[1]
    ys_ref[...] = y[:short_rows].reshape(ys_ref.shape)
    yl_ref[0] = y[short_rows:]


def call(kernel, name, out, ins, scratch=(), flops=10**8, moved=10**6, **kw):
    many = isinstance(out, (tuple, list))
    return pl.pallas_call(
        kernel,
        out_shape=out,
        in_specs=ins,
        out_specs=[VMEM] * len(out) if many else VMEM,
        scratch_shapes=list(scratch),
        name=name,
        cost_estimate=pl.CostEstimate(flops=flops, bytes_accessed=moved, transcendentals=0),
        compiler_params=pltpu.CompilerParams(vmem_limit_bytes=48 << 20),
        **kw,
    )


def shape(dims, dtype=BF16):
    return jax.ShapeDtypeStruct(dims, dtype)


def local(
    x_short,
    x_long,
    parents,
    long_parents,
    short_len,
    long_len,
    doc_ids,
    long_doc,
    short_kv,
    long_kv,
    enc_kv,
    w_qkv,
    w_out,
    w_cross_q,
    w_cross_out,
    w_up,
    w_down,
):
    requests, rows, model = x_short.shape
    width = w_qkv.shape[2]
    heads = width // HD
    short_rows = requests * rows
    all_rows = short_rows + rows
    seqs = lax.axis_size("seq")
    reqs = lax.axis_size("req")
    tps = lax.axis_size("tp")
    pairs = reqs // CORES
    pay = width + LANES
    span = enc_kv.shape[2]
    both = ("req", "seq")

    def seq_shift(x, k):
        return lax.ppermute(x, "seq", [(i, (i + k) % seqs) for i in range(seqs)])

    def yz_shift(x, dy, dz):
        perm = []
        for y in range(pairs):
            for c in range(CORES):
                for z in range(seqs):
                    to = ((y + dy) % pairs * CORES + c) * seqs + (z + dz) % seqs
                    perm.append(((y * CORES + c) * seqs + z, to))
        return lax.ppermute(x, both, perm)

    def tp_swap(x):
        return lax.ppermute(x, "tp", [(i, (i + 1) % tps) for i in range(tps)])

    other_kv = lax.ppermute(enc_kv, "req", [(i, i ^ 1) for i in range(reqs)])

    qkv, long_pay = call(
        qkv_kernel,
        "qkv",
        (shape((3, all_rows, width)), shape((rows, pay))),
        [SMEM] + [VMEM] * 4,
    )(long_len, x_short, x_long, w_qkv, long_kv)
    got = [seq_shift(long_pay, k) for k in range(1, seqs)]
    partial = call(
        functools.partial(attend_kernel, seqs - 1),
        "attend",
        shape((all_rows, model)),
        [SMEM] + [VMEM] * (5 + seqs),
        [pltpu.VMEM((all_rows, width), BF16), pltpu.VMEM((seqs, rows, pay), BF16)],
    )(short_len, parents, long_parents, qkv, short_kv, w_out, long_pay, *got)

    hidden_one, q_long, q_short = call(
        query_kernel,
        "query",
        (shape((all_rows, model)), shape((rows, width)), shape((short_rows, width))),
        [VMEM] * 5,
    )(x_short, x_long, partial, tp_swap(partial), w_cross_q)

    own_q = jnp.concatenate([q_short] + [seq_shift(q_short, k) for k in range(1, seqs)] + [q_long])
    entries = seqs * requests + 1
    req = lax.axis_index("req").astype(jnp.int32)

    def cross(dy, q):
        y = (req // CORES - dy + pairs) % pairs
        group = (y * CORES + req % CORES).reshape(1)
        return call(
            functools.partial(cross_kernel, seqs, requests),
            "cross",
            shape((seqs, all_rows, pay)),
            [SMEM] * 3 + [ANY] * 2 + [VMEM],
            [
                pltpu.VMEM((entries, 2, CORES * span, width), BF16),
                pltpu.SemaphoreType.DMA((entries, 2)),
            ],
        )(group, doc_ids, long_doc, enc_kv, other_kv, q)

    pieces, places = [], []
    for dy in range(pairs):
        out = cross(dy, own_q if dy == 0 else yz_shift(own_q, dy, 0))
        for k in range(seqs):
            block = out[k]
            if (dy, k) != (0, 0):
                block = yz_shift(block, -dy, -k)
            pieces.append(block)
            places.append(((-dy) % pairs, k))
    partial = call(
        functools.partial(merge_kernel, tuple(places), seqs),
        "merge",
        shape((all_rows, model)),
        [VMEM] * (1 + len(pieces)),
        [pltpu.VMEM((len(pieces), all_rows, pay), BF16), pltpu.VMEM((all_rows, width), BF16)],
    )(w_cross_out, *pieces)

    hidden = w_up.shape[1]
    block = 512
    whole = pl.BlockSpec((all_rows, model), lambda i: (0, 0))
    hidden_two, partial = pl.pallas_call(
        ffn_kernel,
        grid=(hidden // block,),
        out_shape=(shape((all_rows, model)), shape((all_rows, model))),
        in_specs=[
            whole,
            whole,
            whole,
            pl.BlockSpec((model, block), lambda i: (0, i)),
            pl.BlockSpec((block, model), lambda i: (i, 0)),
        ],
        out_specs=(whole, whole),
        scratch_shapes=[pltpu.VMEM((all_rows, model), F32)],
        name="ffn",
        compiler_params=pltpu.CompilerParams(
            dimension_semantics=("arbitrary",), vmem_limit_bytes=48 << 20
        ),
    )(hidden_one, partial, tp_swap(partial), w_up, w_down)

    return call(
        final_kernel,
        "final",
        (shape((requests, rows, model)), shape((1, rows, model))),
        [VMEM] * 3,
    )(hidden_two, partial, tp_swap(partial))


def solution(mesh):
    in_specs = (
        P(("req", "seq"), None, None),
        P("req", None, None),
        P(("req", "seq"), None),
        P("req", None),
        P(("req", "seq")),
        P("req"),
        P(),
        P(),
        P(("req", "seq"), None, None, "tp"),
        P("req", None, "seq", "tp"),
        P(None, None, ("req", "seq"), "tp"),
        P(None, None, "tp"),
        P("tp", None),
        P(None, "tp"),
        P("tp", None),
        P(None, "tp"),
        P("tp", None),
    )
    out_specs = (P(("req", "seq"), None, None), P("req", None, None))
    return jax.shard_map(local, mesh=mesh, in_specs=in_specs, out_specs=out_specs, check_vma=False)
```

```python
import functools

import jax
import jax.numpy as jnp
from jax import lax
from jax.experimental import pallas as pl
from jax.experimental.pallas import tpu as pltpu
from jax.sharding import PartitionSpec as P

HD = 64
LANES = 128
CORES = 2
PIECES = 3
SLOTS = 4
MASKED = -1e30
EPS = 1e-05
F32 = jnp.float32
BF16 = jnp.bfloat16
VMEM = pl.BlockSpec(memory_space=pltpu.VMEM)
SMEM = pl.BlockSpec(memory_space=pltpu.SMEM)
HBM = pl.BlockSpec(memory_space=pltpu.HBM)


def iota(shape, axis):
    return lax.broadcasted_iota(jnp.int32, shape, axis)


def dot(a, b):
    return lax.dot_general(a, b, (((1,), (0,)), ((), ())), preferred_element_type=F32)


def dot_t(a, b):
    return lax.dot_general(a, b, (((1,), (1,)), ((), ())), preferred_element_type=F32)


def normalize(v):
    centered = v - jnp.mean(v, axis=-1, keepdims=True)
    return centered * lax.rsqrt(jnp.mean(centered * centered, axis=-1, keepdims=True) + EPS)


def halves(rows, dtype):
    low = (iota((rows, LANES), 1) < HD).astype(F32)
    return low.astype(dtype), (1.0 - low).astype(dtype)


def scores_of(q, k):
    rows, width = q.shape
    low, high = halves(rows, BF16)
    parts = []
    for at in range(0, width, LANES):
        tile = q[:, at : at + LANES]
        pair = jnp.concatenate([tile * low, tile * high], axis=0)
        parts.append(dot_t(pair, k[:, at : at + LANES]))
    return jnp.concatenate(parts, axis=0) * HD ** (-0.5)


def values_of(p, v):
    width = v.shape[1]
    rows = p.shape[0] * HD // width
    low = iota((rows, LANES), 1) < HD
    p = p.astype(BF16)
    parts = []
    for at in range(0, width, LANES):
        row = at // HD * rows
        o = dot(p[row : row + 2 * rows], v[:, at : at + LANES])
        parts.append(jnp.where(low, o[:rows], o[rows:]))
    return jnp.concatenate(parts, axis=1)


def pack_stats(lse, heads, group):
    rows = lse.shape[0] // heads
    lane = iota((rows, LANES), 1)
    spread = jnp.zeros((rows, LANES), F32)
    for h in range(heads):
        spread = jnp.where(lane % heads == h, lse[h * rows : (h + 1) * rows], spread)
    high = spread.astype(BF16).astype(F32)
    rest = spread - high
    mid = rest.astype(BF16).astype(F32)
    low = (rest - mid).astype(BF16).astype(F32)
    place = lane // heads
    base = group * SLOTS
    packed = jnp.where(place == base, high, 0.0)
    packed = jnp.where(place == base + 1, mid, packed)
    return jnp.where(place == base + 2, low, packed)


def expand_stats(stats, heads, group=0):
    width = heads * HD
    lane = iota((LANES, width), 0)
    place = lane // heads - group * SLOTS
    hot = jnp.logical_and(lane % heads == iota((LANES, width), 1) // HD, place >= 0)
    hot = jnp.logical_and(hot, place < PIECES)
    return dot(stats, hot.astype(F32).astype(BF16))


def softmax_part(s, allowed):
    if allowed is not None:
        s = jnp.where(allowed, s, MASKED)
    m = jnp.max(s, axis=-1, keepdims=True)
    p = jnp.exp(s - m)
    if allowed is not None:
        p = jnp.where(allowed, p, 0.0)
    l = jnp.maximum(jnp.sum(p, axis=-1, keepdims=True), 1e-30)
    return p * (1.0 / l), m + jnp.log(l)


def merge(values, scores):
    top = functools.reduce(jnp.maximum, scores)
    total = acc = None
    for value, score in zip(values, scores):
        w = jnp.exp(score - top)
        total = w if total is None else total + w
        acc = w * value if acc is None else acc + w * value
    return acc / total


def ancestors(parents):
    rows = parents.shape[1]
    node_j = iota((rows, rows), 0)
    node_i = iota((rows, rows), 1)
    eye = (node_i == node_j).astype(F32)
    hot = jnp.logical_and(parents == node_j, node_i > 0).astype(F32)
    closure = eye + hot
    reach = 1
    while reach < rows:
        b = closure.astype(BF16)
        closure = jnp.minimum(dot(b, b), 1.0)
        reach *= 2
    return lax.dot_general(
        closure.astype(BF16),
        eye.astype(BF16),
        (((0,), (0,)), ((), ())),
        preferred_element_type=F32,
    )


def qkv_kernel(*refs):
    ins, outs, rest = refs[:8], refs[8:13], refs[13:]
    qkv_ref, x_ref, pay_ref, tree_ref, allow_ref = outs
    held, sems, ll = rest[:7], rest[7], ins[7]
    xs, xl, w, kv, ps, lp, sl = held
    copies = [
        pltpu.make_async_copy(a, b, sems.at[i])
        for i, (a, b) in enumerate(zip(ins, held))
        if i != 2
    ]
    w_copies = [
        pltpu.make_async_copy(ins[2].at[m], w.at[m], sems.at[7 + m]) for m in range(3)
    ]
    for copy in copies[4:] + copies[:2] + w_copies + copies[2:4]:
        copy.start()
    requests, short, model = xs.shape
    short_rows = requests * short
    rows = xl.shape[1]
    width = w.shape[2]
    heads = width // HD
    for copy in copies[3:]:
        copy.wait()
    for j in range(requests):
        tree_ref[j] = ancestors(ps[j : j + 1, :])
        allow_ref[j : j + 1, :] = (iota((1, allow_ref.shape[1]), 1) < sl[j]).astype(F32)
    tree_ref[requests] = ancestors(lp[...])
    for copy in copies[:2]:
        copy.wait()
    x = jnp.concatenate([xs[...].reshape(short_rows, model), xl[0]], axis=0)
    x_ref[...] = x
    for m in range(3):
        w_copies[m].wait()
        qkv_ref[m] = dot(x, w[m]).astype(BF16)
    copies[2].wait()
    span = kv.shape[2]
    allowed = iota((1, span), 1) + lax.axis_index("seq") * span < ll[0]
    s = scores_of(qkv_ref[0, short_rows:, :], kv[0, 0])
    p, lse = softmax_part(s, allowed)
    pay_ref[:, :width] = values_of(p, kv[0, 1]).astype(BF16)
    pay_ref[:, width:] = pack_stats(lse, heads, 0).astype(BF16)


def attend_kernel(qkv_ref, skv_ref, tree_ref, allow_ref, attn_ref, draft_ref, stat_ref):
    requests, _, span, width = skv_ref.shape
    heads = width // HD
    rows = tree_ref.shape[1]
    for j in range(requests):
        part = slice(j * rows, (j + 1) * rows)
        q = qkv_ref[0, part, :]
        allowed = allow_ref[j : j + 1, :] > 0.5
        allowed_d = jnp.concatenate([tree_ref[j]] * heads, axis=0) > 0.5
        s = jnp.where(allowed, scores_of(q, skv_ref[j, 0]), MASKED)
        d = jnp.where(allowed_d, scores_of(q, qkv_ref[1, part, :]), MASKED)
        m = jnp.maximum(jnp.max(s, axis=-1, keepdims=True), jnp.max(d, axis=-1, keepdims=True))
        p = jnp.where(allowed, jnp.exp(s - m), 0.0)
        pd = jnp.where(allowed_d, jnp.exp(d - m), 0.0)
        l = jnp.sum(p, axis=-1, keepdims=True) + jnp.sum(pd, axis=-1, keepdims=True)
        inverse = 1.0 / l
        o = values_of(p * inverse, skv_ref[j, 1]) + values_of(pd * inverse, qkv_ref[2, part, :])
        attn_ref[part, :] = o.astype(BF16)
    row = requests * rows
    allowed = jnp.concatenate([tree_ref[requests]] * heads, axis=0) > 0.5
    p, lse = softmax_part(scores_of(qkv_ref[0, row:, :], qkv_ref[1, row:, :]), allowed)
    draft_ref[...] = values_of(p, qkv_ref[2, row:, :])
    stat_ref[...] = pack_stats(lse, heads, 0).astype(BF16)


def output_kernel(hops, attn_ref, draft_ref, stat_ref, wo_ref, *rest):
    pay_refs, (out_ref, attn, pays) = rest[: hops + 1], rest[hops + 1 :]
    short_rows, width = attn_ref.shape
    heads = width // HD
    zed = lax.axis_index("seq")
    seqs = hops + 1
    for hop in range(seqs):
        pays[lax.rem(zed - hop + seqs, seqs)] = pay_refs[hop][...]
    values = [draft_ref[...]] + [pays[z, :, :width].astype(F32) for z in range(seqs)]
    scores = [expand_stats(stat_ref[...], heads)] + [
        expand_stats(pays[z, :, width:], heads) for z in range(seqs)
    ]
    attn[:short_rows, :] = attn_ref[...]
    attn[short_rows:, :] = merge(values, scores).astype(BF16)
    out_ref[...] = dot(attn[...], wo_ref[...]).astype(BF16)


def query_kernel(x_ref, a_ref, b_ref, w_ref, h_ref, q_ref, qs_ref):
    short_rows = qs_ref.shape[0]
    x = x_ref[...].astype(F32)
    h = normalize(x + (a_ref[...].astype(F32) + b_ref[...].astype(F32))).astype(BF16)
    h_ref[...] = h
    q = dot(h, w_ref[...]).astype(BF16)
    q_ref[...] = q[short_rows:]
    qs_ref[...] = q[:short_rows]


def fetch_kernel(seqs, requests, dys, doc_ref, long_ref, own_ref, other_ref, *rest):
    outs, sems = rest[: len(dys)], rest[len(dys)]
    span = own_ref.shape[2]
    short_total = seqs * requests
    zed = lax.axis_index("seq")
    req = lax.axis_index("req")
    pairs = lax.axis_size("req") // CORES
    for at, dy in enumerate(dys):
        group = lax.rem(req // CORES - dy + pairs, pairs) * CORES + lax.rem(req, CORES)
        kv = outs[at]
        copies = []
        for e in range(short_total + 1):
            if e == short_total:
                doc = long_ref[group]
            else:
                place = lax.rem(zed - e // requests + seqs, seqs)
                doc = doc_ref[(group * seqs + place) * requests + e % requests]
            for half, ref in enumerate((own_ref, other_ref)):
                copies.append(
                    pltpu.make_async_copy(
                        ref.at[:, doc],
                        kv.at[e, :, pl.ds(half * span, span)],
                        sems.at[at, e, half],
                    )
                )
                copies[-1].start()
        if at == 0:
            first = copies
        else:
            first = first + copies
    for copy in first:
        copy.wait()


def cross_kernel(seqs, requests, kv_ref, q_ref, *pay_refs):
    all_rows = q_ref.shape[0]
    width = q_ref.shape[1]
    heads = width // HD
    short_total = seqs * requests
    rows = all_rows // (short_total + 1)
    pay_rows = (requests + 1) * rows

    def one(e, group):
        s = scores_of(q_ref[e * rows : (e + 1) * rows, :], kv_ref[e, 0])
        p, lse = softmax_part(s, None)
        return values_of(p, kv_ref[e, 1]).astype(BF16), pack_stats(lse, heads, group)

    long_o, long_stats = one(short_total, requests)
    for k in range(seqs):
        stats = long_stats
        for j in range(requests):
            o, more = one(k * requests + j, j)
            stats = stats + more
            pay_refs[k][j * rows : (j + 1) * rows, :] = o
        pay_refs[k][requests * rows : pay_rows, :] = long_o
        for at in range(0, rows, 8):
            lanes = slice(at // 8 * LANES, (at // 8 + 1) * LANES)
            pay_refs[k][pay_rows:, lanes] = stats[at : at + 8].astype(BF16)


def merge_kernel(places, seqs, w_ref, *rest):
    ins, (out_ref, pays, cross) = rest[: len(places)], rest[len(places) :]
    all_rows, width = cross.shape
    heads = width // HD
    pairs = lax.axis_size("req") // CORES
    yed = lax.axis_index("req") // CORES
    zed = lax.axis_index("seq")
    for ref, (dy, dz) in zip(ins, places):
        at = lax.rem(yed - dy + pairs, pairs) * seqs + lax.rem(zed + dz, seqs)
        pays[at] = ref[...]
    stats = []
    for s in range(len(places)):
        block = pays[s, all_rows:, :].astype(F32)
        tiles = [block[:, at : at + LANES] for at in range(0, width, LANES)]
        stats.append(jnp.concatenate(tiles, axis=0).astype(BF16))
    step = 8 * width // LANES
    for group in range(all_rows // step):
        part = slice(group * step, (group + 1) * step)
        values = [pays[s, part, :].astype(F32) for s in range(len(places))]
        scores = [expand_stats(stats[s], heads, group) for s in range(len(places))]
        cross[part, :] = merge(values, scores).astype(BF16)
    out_ref[...] = dot(cross[...], w_ref[...]).astype(BF16)


def gelu(x):
    return 0.5 * x * (1.0 + lax.erf(x * 0.5**0.5))


def ffn_kernel(h_ref, a_ref, b_ref, up_ref, down_ref, h2_ref, out_ref):
    total = h_ref[...].astype(F32) + (a_ref[...].astype(F32) + b_ref[...].astype(F32))
    h2 = normalize(total).astype(BF16)
    h2_ref[...] = h2
    acc = None
    for at in range(0, up_ref.shape[1], 512):
        act = gelu(dot(h2, up_ref[:, at : at + 512])).astype(BF16)
        part = dot(act, down_ref[at : at + 512, :])
        acc = part if acc is None else acc + part
    out_ref[...] = acc.astype(BF16)


def final_kernel(h_ref, a_ref, b_ref, ys_ref, yl_ref):
    total = h_ref[...].astype(F32) + (a_ref[...].astype(F32) + b_ref[...].astype(F32))
    y = normalize(total).astype(BF16)
    short_rows = ys_ref.shape[0] * ys_ref.shape[1]
    ys_ref[...] = y[:short_rows].reshape(ys_ref.shape)
    yl_ref[0] = y[short_rows:]


def call(kernel, name, out, ins, scratch=(), flops=10**8, moved=10**6, grant=16 << 20):
    many = isinstance(out, (tuple, list))
    return pl.pallas_call(
        kernel,
        out_shape=out,
        in_specs=ins,
        out_specs=[VMEM] * len(out) if many else VMEM,
        scratch_shapes=list(scratch),
        name=name,
        cost_estimate=pl.CostEstimate(flops=flops, bytes_accessed=moved, transcendentals=0),
        compiler_params=pltpu.CompilerParams(vmem_limit_bytes=grant),
    )


def in_hbm(x):
    return pltpu.with_memory_space_constraint(x, pltpu.HBM)


def shape(dims, dtype=BF16):
    return jax.ShapeDtypeStruct(dims, dtype)


def local(
    x_short,
    x_long,
    parents,
    long_parents,
    short_len,
    long_len,
    doc_ids,
    long_doc,
    short_kv,
    long_kv,
    enc_kv,
    w_qkv,
    w_out,
    w_cross_q,
    w_cross_out,
    w_up,
    w_down,
):
    requests, rows, model = x_short.shape
    width = w_qkv.shape[2]
    heads = width // HD
    short_rows = requests * rows
    all_rows = short_rows + rows
    seqs = lax.axis_size("seq")
    reqs = lax.axis_size("req")
    tps = lax.axis_size("tp")
    pairs = reqs // CORES
    pay = width + LANES
    span = enc_kv.shape[2]
    both = ("req", "seq")

    def seq_shift(x, k):
        return lax.ppermute(x, "seq", [(i, (i + k) % seqs) for i in range(seqs)])

    def yz_shift(x, dy, dz):
        perm = []
        for y in range(pairs):
            for c in range(CORES):
                for z in range(seqs):
                    to = ((y + dy) % pairs * CORES + c) * seqs + (z + dz) % seqs
                    perm.append(((y * CORES + c) * seqs + z, to))
        return lax.ppermute(x, both, perm)

    def tp_swap(x):
        return lax.ppermute(x, "tp", [(i, (i + 1) % tps) for i in range(tps)])

    other_kv = lax.ppermute(enc_kv, "req", [(i, i ^ 1) for i in range(reqs)])

    qkv, inputs, long_pay, tree, allow = call(
        qkv_kernel,
        "qkv",
        (
            shape((3, all_rows, width)),
            shape((all_rows, model)),
            shape((rows, pay)),
            shape((requests + 1, rows, rows), F32),
            shape((requests, short_kv.shape[2]), F32),
        ),
        [HBM] * 7 + [SMEM],
        [
            pltpu.VMEM(x_short.shape, BF16),
            pltpu.VMEM(x_long.shape, BF16),
            pltpu.VMEM(w_qkv.shape, BF16),
            pltpu.VMEM(long_kv.shape, BF16),
            pltpu.VMEM(parents.shape, jnp.int32),
            pltpu.VMEM(long_parents.shape, jnp.int32),
            pltpu.SMEM(short_len.shape, jnp.int32),
            pltpu.SemaphoreType.DMA((10,)),
        ],
    )(
        *map(in_hbm, (x_short, x_long, w_qkv, long_kv, parents, long_parents, short_len)), long_len
    )
    got = [seq_shift(long_pay, k) for k in range(1, seqs)]
    attn, draft, stats = call(
        attend_kernel,
        "attend",
        (shape((short_rows, width)), shape((rows, width), F32), shape((rows, LANES))),
        [VMEM] * 4,
    )(qkv, short_kv, tree, allow)
    partial = call(
        functools.partial(output_kernel, seqs - 1),
        "output",
        shape((all_rows, model)),
        [VMEM] * (4 + seqs),
        [pltpu.VMEM((all_rows, width), BF16), pltpu.VMEM((seqs, rows, pay), BF16)],
    )(attn, draft, stats, w_out, long_pay, *got)

    hidden_one, q_long, q_short = call(
        query_kernel,
        "query",
        (shape((all_rows, model)), shape((rows, width)), shape((short_rows, width))),
        [VMEM] * 4,
    )(inputs, partial, tp_swap(partial), w_cross_q)

    shifted = [q_short] + [seq_shift(q_short, k) for k in range(1, seqs)]
    entries = seqs * requests + 1
    dys = tuple(range(pairs))
    docs, _ = lax.optimization_barrier((doc_ids, q_short))
    kvs = call(
        functools.partial(fetch_kernel, seqs, requests, dys),
        "fetch",
        tuple(shape((entries, 2, CORES * span, width)) for _ in dys),
        [SMEM] * 2 + [HBM] * 2,
        [pltpu.SemaphoreType.DMA((pairs, entries, 2))],
        flops=4 * 10**9,
    )(docs, long_doc, in_hbm(enc_kv), other_kv)
    shifted, kvs = lax.optimization_barrier((shifted, kvs))
    own_q = jnp.concatenate(shifted + [q_long])
    pay_rows = all_rows + rows * LANES // width

    pieces, places = [], []
    for dy in dys:
        q = own_q
        if dy:
            q, *done = lax.optimization_barrier((yz_shift(own_q, dy, 0), *out))
        out = call(
            functools.partial(cross_kernel, seqs, requests),
            "cross",
            [shape((pay_rows, width))] * seqs,
            [VMEM] * 2,
            flops=4 * 10**9,
        )(kvs[dy], q)
        for k in range(seqs):
            block = out[k]
            if (dy, k) != (0, 0):
                block = yz_shift(block, -dy, -k)
            pieces.append(block)
            places.append(((-dy) % pairs, k))
    partial = call(
        functools.partial(merge_kernel, tuple(places), seqs),
        "merge",
        shape((all_rows, model)),
        [VMEM] * (1 + len(pieces)),
        [pltpu.VMEM((len(pieces), pay_rows, width), BF16), pltpu.VMEM((all_rows, width), BF16)],
    )(w_cross_out, *pieces)

    hidden_two, partial = call(
        ffn_kernel, "ffn", (shape((all_rows, model)),) * 2, [VMEM] * 5
    )(hidden_one, partial, tp_swap(partial), w_up, w_down)

    return call(
        final_kernel,
        "final",
        (shape((requests, rows, model)), shape((1, rows, model))),
        [VMEM] * 3,
    )(hidden_two, partial, tp_swap(partial))


def solution(mesh):
    in_specs = (
        P(("req", "seq"), None, None),
        P("req", None, None),
        P(("req", "seq"), None),
        P("req", None),
        P(("req", "seq")),
        P("req"),
        P(),
        P(),
        P(("req", "seq"), None, None, "tp"),
        P("req", None, "seq", "tp"),
        P(None, None, ("req", "seq"), "tp"),
        P(None, None, "tp"),
        P("tp", None),
        P(None, "tp"),
        P("tp", None),
        P(None, "tp"),
        P("tp", None),
    )
    out_specs = (P(("req", "seq"), None, None), P("req", None, None))
    return jax.shard_map(local, mesh=mesh, in_specs=in_specs, out_specs=out_specs, check_vma=False)
```

```python
import functools

import jax
import jax.numpy as jnp
from jax import lax
from jax.experimental import pallas as pl
from jax.experimental.pallas import tpu as pltpu
from jax.sharding import PartitionSpec as P

HD = 64
LANES = 128
CORES = 2
PIECES = 3
SLOTS = 4
MASKED = -1e30
EPS = 1e-05
F32 = jnp.float32
BF16 = jnp.bfloat16
VMEM = pl.BlockSpec(memory_space=pltpu.VMEM)
SMEM = pl.BlockSpec(memory_space=pltpu.SMEM)
HBM = pl.BlockSpec(memory_space=pltpu.HBM)


def iota(shape, axis):
    return lax.broadcasted_iota(jnp.int32, shape, axis)


def dot(a, b):
    return lax.dot_general(a, b, (((1,), (0,)), ((), ())), preferred_element_type=F32)


def dot_t(a, b):
    return lax.dot_general(a, b, (((1,), (1,)), ((), ())), preferred_element_type=F32)


def normalize(v):
    centered = v - jnp.mean(v, axis=-1, keepdims=True)
    return centered * lax.rsqrt(jnp.mean(centered * centered, axis=-1, keepdims=True) + EPS)


def halves(rows, dtype):
    low = (iota((rows, LANES), 1) < HD).astype(F32)
    return low.astype(dtype), (1.0 - low).astype(dtype)


def scores_of(q, k):
    rows, width = q.shape
    low, high = (half * HD ** (-0.5) for half in halves(rows, BF16))
    parts = []
    for at in range(0, width, LANES):
        tile = q[:, at : at + LANES]
        pair = jnp.concatenate([tile * low, tile * high], axis=0)
        parts.append(dot_t(pair, k[:, at : at + LANES]))
    return jnp.concatenate(parts, axis=0)


def sums_of(p):
    return dot(p, jnp.ones((p.shape[1], LANES), BF16))


def values_of(terms, total):
    width = terms[0][1].shape[1]
    rows = total.shape[0] * HD // width
    low = iota((rows, LANES), 1) < HD
    parts = []
    for at in range(0, width, LANES):
        row = at // HD * rows
        mid, end = row + rows, row + 2 * rows
        o = sum(dot(p[row:end], v[:, at : at + LANES]) for p, v in terms)
        o = jnp.where(low, o[:rows], o[rows:])
        parts.append(o / jnp.where(low, total[row:mid], total[mid:end]))
    return jnp.concatenate(parts, axis=1)


def spread(columns, heads):
    rows = columns.shape[0] // heads
    lane = iota((rows, LANES), 1) % heads
    out = jnp.zeros((rows, LANES), F32)
    for h in range(heads):
        out = jnp.where(lane == h, columns[h * rows : (h + 1) * rows], out)
    return out


def pack_stats(lse, heads, group=None):
    place = iota(lse.shape, 1) // heads
    if group is None:
        group, place = 0, place % SLOTS
    high = lse.astype(BF16).astype(F32)
    rest = lse - high
    mid = rest.astype(BF16).astype(F32)
    low = (rest - mid).astype(BF16).astype(F32)
    base = group * SLOTS
    packed = jnp.where(place == base, high, 0.0)
    packed = jnp.where(place == base + 1, mid, packed)
    return jnp.where(place == base + 2, low, packed)


def piece_hot(heads, group, shape, per_head):
    lane = iota(shape, 0)
    place = lane // heads - group * SLOTS
    hot = jnp.logical_and(lane % heads == per_head, place >= 0)
    return jnp.logical_and(hot, place < PIECES).astype(F32).astype(BF16)


def expand_stats(stats, heads, group=0):
    shape = (LANES, heads * HD)
    return dot(stats, piece_hot(heads, group, shape, iota(shape, 1) // HD))


def respread(stats, heads):
    shape = (LANES, LANES)
    return dot(stats, piece_hot(heads, 0, shape, iota(shape, 1) % heads))


def softmax_part(s, v, heads, allowed=None):
    if allowed is not None:
        s = jnp.where(allowed, s, MASKED)
    m = jnp.max(s, axis=-1, keepdims=True)
    p = jnp.exp(s - m)
    if allowed is not None:
        p = jnp.where(allowed, p, 0.0)
    p = p.astype(BF16)
    l = jnp.maximum(sums_of(p), 1e-30)
    return values_of([(p, v)], l), spread(m, heads) + jnp.log(spread(l, heads))


def merge(values, scores):
    top = functools.reduce(jnp.maximum, scores)
    total = acc = None
    for value, score in zip(values, scores):
        w = jnp.exp(score - top)
        total = w if total is None else total + w
        acc = w * value if acc is None else acc + w * value
    return acc / total


def ancestors(parents, rows):
    nodes = parents.shape[1]
    node_j = iota((nodes, nodes), 0)
    node_i = iota((nodes, nodes), 1)
    target = parents + node_i // rows * rows
    hot = jnp.logical_and(target == node_j, node_i % rows > 0).astype(F32)
    closure = (node_i == node_j).astype(F32) + hot
    reach = 1
    while reach < rows:
        b = closure.astype(BF16)
        closure = jnp.minimum(dot(b, b), 1.0)
        reach *= 2
    shape = (nodes, rows)
    place = (iota(shape, 0) % rows == iota(shape, 1)).astype(F32)
    return lax.dot_general(
        closure.astype(BF16),
        place.astype(BF16),
        (((0,), (0,)), ((), ())),
        preferred_element_type=F32,
    )


def first_kernel(
    xs_hbm, xl_hbm, w_hbm, kv_hbm, ps_hbm, lp_hbm, q_ref, x_ref, kv_ref, tree_ref, w, ps, lp, sems
):
    requests, rows, model = xs_hbm.shape
    short_rows = requests * rows
    moves = [(ps_hbm, ps), (lp_hbm, lp)]
    moves += [(xs_hbm.at[j], x_ref.at[pl.ds(j * rows, rows)]) for j in range(requests)]
    moves += [(xl_hbm.at[0], x_ref.at[pl.ds(short_rows, rows)]), (w_hbm.at[0], w)]
    moves += [(kv_hbm.at[0], kv_ref)]
    copies = [pltpu.make_async_copy(a, b, sems.at[i]) for i, (a, b) in enumerate(moves)]
    for copy in copies:
        copy.start()
    for copy in copies[:2]:
        copy.wait()
    parents = [ps[j : j + 1, :] for j in range(requests)] + [lp[...]]
    tree_ref[...] = ancestors(jnp.concatenate(parents, axis=1), rows)
    for copy in copies[2:-1]:
        copy.wait()
    q_ref[...] = dot(x_ref[...], w[...]).astype(BF16)
    copies[-1].wait()


def long_kernel(q_ref, kv_ref, len_ref, pay_ref):
    rows = pay_ref.shape[0]
    width = q_ref.shape[1]
    heads = width // HD
    span = kv_ref.shape[1]
    allowed = iota((1, span), 1) + lax.axis_index("seq") * span < len_ref[:, :1]
    s = scores_of(q_ref[q_ref.shape[0] - rows :, :], kv_ref[0])
    o, lse = softmax_part(s, kv_ref[1], heads, allowed)
    pay_ref[:, :width] = o.astype(BF16)
    pay_ref[:, width:] = pack_stats(lse, heads, 0).astype(BF16)


def short_attend(q, k, v, cache_k, cache_v, allowed, tree, heads):
    allowed_d = jnp.concatenate([tree] * heads, axis=0) > 0.5
    s = jnp.where(allowed, scores_of(q, cache_k), MASKED)
    d = jnp.where(allowed_d, scores_of(q, k), MASKED)
    m = jnp.maximum(jnp.max(s, axis=-1, keepdims=True), jnp.max(d, axis=-1, keepdims=True))
    p = jnp.exp(s - m).astype(BF16)
    pd = jnp.exp(d - m).astype(BF16)
    return values_of([(p, cache_v), (pd, v)], sums_of(p) + sums_of(pd)).astype(BF16)


def attend_kernel(
    q_ref, x_ref, w_ref, skv_ref, tree_ref, sl_hbm, attn_ref, draft_ref, stat_ref, sl, sem
):
    requests = skv_ref.shape[0]
    rows = tree_ref.shape[1]
    copy = pltpu.make_async_copy(sl_hbm, sl, sem.at[0])
    copy.start()
    heads = q_ref.shape[1] // HD
    span = skv_ref.shape[2]
    x = x_ref[...]
    k = dot(x, w_ref[1]).astype(BF16)
    v = dot(x, w_ref[2]).astype(BF16)
    row = requests * rows
    allowed = jnp.concatenate([tree_ref[row:, :]] * heads, axis=0) > 0.5
    s = scores_of(q_ref[row:, :], k[row:])
    o, lse = softmax_part(s, v[row:], heads, allowed)
    draft_ref[...] = o
    stat_ref[...] = pack_stats(lse, heads, 0).astype(BF16)
    copy.wait()
    for j in range(requests):
        part = slice(j * rows, (j + 1) * rows)
        attn_ref[part, :] = short_attend(
            q_ref[part, :], k[part], v[part], skv_ref[j, 0], skv_ref[j, 1],
            iota((1, span), 1) < sl[j], tree_ref[part, :], heads,
        )


def output_kernel(hops, attn_ref, draft_ref, stat_ref, wo_ref, *rest):
    pay_refs, (out_ref, attn, pays) = rest[: hops + 1], rest[hops + 1 :]
    short_rows, width = attn_ref.shape
    heads = width // HD
    zed = lax.axis_index("seq")
    for hop, ref in enumerate(pay_refs):
        pays[zed ^ hop] = ref[...]
    values = [draft_ref[...]] + [pays[z, :, :width].astype(F32) for z in range(hops + 1)]
    scores = [expand_stats(stat_ref[...], heads)] + [
        expand_stats(pays[z, :, width:], heads) for z in range(hops + 1)
    ]
    attn[:short_rows, :] = attn_ref[...]
    attn[short_rows:, :] = merge(values, scores).astype(BF16)
    out_ref[...] = dot(attn[...], wo_ref[...]).astype(BF16)


def query_kernel(x_ref, a_ref, b_ref, w_ref, h_ref, q_ref, qs_ref):
    short_rows = qs_ref.shape[0]
    x = x_ref[...].astype(F32)
    h = normalize(x + (a_ref[...].astype(F32) + b_ref[...].astype(F32))).astype(BF16)
    h_ref[...] = h
    q = dot(h, w_ref[...]).astype(BF16)
    q_ref[...] = q
    qs_ref[...] = q[:short_rows]


def fetch_kernel(seqs, requests, dys, doc_ref, long_ref, own_ref, other_ref, *rest):
    outs, sems = rest[: len(dys)], rest[len(dys)]
    span = own_ref.shape[2]
    short_total = seqs * requests
    zed = lax.axis_index("seq")
    req = lax.axis_index("req")
    pairs = lax.axis_size("req") // CORES
    for at, dy in enumerate(dys):
        group = lax.rem(req // CORES - dy + pairs, pairs) * CORES + lax.rem(req, CORES)
        kv = outs[at]
        copies = []
        for e in range(short_total + 1):
            if e == short_total:
                doc = long_ref[group]
            else:
                place = zed ^ (e // requests)
                doc = doc_ref[(group * seqs + place) * requests + e % requests]
            for half, ref in enumerate((own_ref, other_ref)):
                copies.append(
                    pltpu.make_async_copy(
                        ref.at[:, doc],
                        kv.at[e, :, pl.ds(half * span, span)],
                        sems.at[at, e, half],
                    )
                )
                copies[-1].start()
        if at == 0:
            first = copies
        else:
            first = first + copies
    for copy in first:
        copy.wait()


def document_part(kv_ref, e, q, heads, group):
    o, lse = softmax_part(scores_of(q, kv_ref[e, 0]), kv_ref[e, 1], heads)
    return o.astype(BF16), pack_stats(lse, heads, group)


def fill(pay_ref, parts, long_o, long_stats):
    rows = long_o.shape[0]
    for j, (o, more) in enumerate(parts):
        pay_ref[j * rows : (j + 1) * rows, :] = o
        long_stats = long_stats + more
    end = (len(parts) + 1) * rows
    pay_ref[end - rows : end, :] = long_o
    write_stats(pay_ref, end, long_stats)


def write_stats(pay_ref, row, stats):
    for at in range(0, stats.shape[0], 8):
        lanes = slice(at // 8 * LANES, (at // 8 + 1) * LANES)
        pay_ref[row : row + 8, lanes] = stats[at : at + 8].astype(BF16)


def read_stats(block):
    block = block.astype(F32)
    tiles = [block[:, at : at + LANES] for at in range(0, block.shape[1], LANES)]
    return jnp.concatenate(tiles, axis=0).astype(BF16)


def near_kernel(requests, kv_ref, q_ref, pay_ref, o_ref, stat_ref):
    rows, width = o_ref.shape
    heads = width // HD
    last = q_ref.shape[0] - rows
    o, stats = document_part(kv_ref, kv_ref.shape[0] - 1, q_ref[last:, :], heads, requests)
    o_ref[...] = o
    stat_ref[...] = stats
    parts = [
        document_part(kv_ref, j, q_ref[j * rows : (j + 1) * rows, :], heads, j)
        for j in range(requests)
    ]
    fill(pay_ref, parts, o, stats)


def row_kernel(requests, stacked, single, kv_ref, o_ref, stat_ref, q_ref, *outs):
    rows, width = o_ref.shape
    heads = width // HD
    targets = [outs[0].at[i] for i in range(len(stacked))]
    targets += outs[1 if stacked else 0 :]
    for k, target in zip(stacked + single, targets):
        parts = []
        for j in range(requests):
            row = ((k - 1) * requests + j) * rows
            q = q_ref[row : row + rows, :]
            parts.append(document_part(kv_ref, k * requests + j, q, heads, j))
        fill(target, parts, o_ref[...], stat_ref[...])


def join(two, out, groups, heads):
    rows, width = out.shape
    step = rows * width // (groups * width + LANES)
    end = groups * step
    lane, other = (iota((LANES, LANES), axis) for axis in range(2))
    slots = heads * SLOTS
    hot = jnp.logical_and(lane % heads == other % heads, lane // slots == other // slots)
    hot = jnp.logical_and(hot, lane // heads % SLOTS < PIECES).astype(F32).astype(BF16)
    stats = [read_stats(two[i, end:, :]) for i in range(2)]
    for group in range(groups):
        part = slice(group * step, (group + 1) * step)
        scores = [expand_stats(x, heads, group) for x in stats]
        out[part, :] = merge([two[i, part, :].astype(F32) for i in range(2)], scores).astype(BF16)
    left, right = (dot(x, hot) for x in stats)
    top = jnp.maximum(left, right)
    lse = top + jnp.log(jnp.exp(left - top) + jnp.exp(right - top))
    write_stats(out, end, pack_stats(lse, heads))


def join_kernel(groups, skip, odd_ref, *rest):
    count = len(rest) // 2
    two = rest[-1]
    heads = two.shape[2] // HD
    odd_z = lax.axis_index("seq") & 1
    for e in range(count):
        two[odd_z] = rest[e][...]
        two[1 - odd_z] = odd_ref[skip + e]
        join(two, rest[count + e], groups, heads)


def merge_kernel(dys, seqs, groups, w_ref, *rest):
    half = seqs // 2
    ins, (out_ref, pays, two, cross) = rest[:-4], rest[-4:]
    all_rows, width = cross.shape
    heads = width // HD
    pairs = lax.axis_size("req") // CORES
    yed = lax.axis_index("req") // CORES
    zed = lax.axis_index("seq")
    odd_z = zed & 1
    per = half + 1
    for at, dy in enumerate(dys):
        zero, one, *far = ins[at * per : (at + 1) * per]
        base = lax.rem(yed + dy, pairs) * half
        two[odd_z] = zero[...]
        two[1 - odd_z] = one[...] if dy else one[0]
        join(two, pays.at[base + zed // 2], groups, heads)
        for e, ref in enumerate(far, 1):
            pays[base + (zed ^ (2 * e)) // 2] = ref[...]
    total = len(dys) * half
    stats = [read_stats(pays[s, all_rows:, :]) for s in range(total)]
    step = all_rows // groups
    for group in range(groups):
        part = slice(group * step, (group + 1) * step)
        values = [pays[s, part, :].astype(F32) for s in range(total)]
        scores = [expand_stats(stats[s], heads, group) for s in range(total)]
        cross[part, :] = merge(values, scores).astype(BF16)
    out_ref[...] = dot(cross[...], w_ref[...]).astype(BF16)


def gelu(x):
    return 0.5 * x * (1.0 + lax.erf(x * 0.5**0.5))


def ffn_kernel(h_ref, a_ref, b_ref, up_ref, down_ref, h2_ref, out_ref):
    total = h_ref[...].astype(F32) + (a_ref[...].astype(F32) + b_ref[...].astype(F32))
    h2 = normalize(total).astype(BF16)
    h2_ref[...] = h2
    acc = None
    for at in range(0, up_ref.shape[1], 512):
        act = gelu(dot(h2, up_ref[:, at : at + 512])).astype(BF16)
        part = dot(act, down_ref[at : at + 512, :])
        acc = part if acc is None else acc + part
    out_ref[...] = acc.astype(BF16)


def final_kernel(h_ref, a_ref, b_ref, ys_ref, yl_ref):
    total = h_ref[...].astype(F32) + (a_ref[...].astype(F32) + b_ref[...].astype(F32))
    y = normalize(total).astype(BF16)
    short_rows = ys_ref.shape[0] * ys_ref.shape[1]
    ys_ref[...] = y[:short_rows].reshape(ys_ref.shape)
    yl_ref[0] = y[short_rows:]


def call(kernel, name, out, ins, scratch=(), flops=10**8, moved=10**6, grant=16 << 20):
    many = isinstance(out, (tuple, list))
    return pl.pallas_call(
        kernel,
        out_shape=out,
        in_specs=ins,
        out_specs=[VMEM] * len(out) if many else VMEM,
        scratch_shapes=list(scratch),
        name=name,
        cost_estimate=pl.CostEstimate(flops=flops, bytes_accessed=moved, transcendentals=0),
        compiler_params=pltpu.CompilerParams(vmem_limit_bytes=grant),
    )


def in_hbm(x):
    return pltpu.with_memory_space_constraint(x, pltpu.HBM)


def shape(dims, dtype=BF16):
    return jax.ShapeDtypeStruct(dims, dtype)


def local(
    x_short,
    x_long,
    parents,
    long_parents,
    short_len,
    long_len,
    doc_ids,
    long_doc,
    short_kv,
    long_kv,
    enc_kv,
    w_qkv,
    w_out,
    w_cross_q,
    w_cross_out,
    w_up,
    w_down,
):
    requests, rows, model = x_short.shape
    width = w_qkv.shape[2]
    heads = width // HD
    short_rows = requests * rows
    all_rows = short_rows + rows
    seqs = lax.axis_size("seq")
    reqs = lax.axis_size("req")
    tps = lax.axis_size("tp")
    pairs = reqs // CORES
    pay = width + LANES
    span = enc_kv.shape[2]
    both = ("req", "seq")

    def seq_pair(x, k):
        return lax.ppermute(x, "seq", [(i, i ^ k) for i in range(seqs)])

    def yz_move(x, dy, dz):
        perm = []
        for y in range(pairs):
            for c in range(CORES):
                for z in range(seqs):
                    to = ((y + dy) % pairs * CORES + c) * seqs + (z ^ dz)
                    perm.append(((y * CORES + c) * seqs + z, to))
        return lax.ppermute(x, both, perm)

    def tp_swap(x):
        return lax.ppermute(x, "tp", [(i, (i + 1) % tps) for i in range(tps)])

    xs, xl, w_hbm, kv_hbm = map(in_hbm, (x_short, x_long, w_qkv, long_kv))
    queries, inputs, cache, tree = call(
        first_kernel,
        "first",
        (
            shape((all_rows, width)),
            shape((all_rows, model)),
            shape(long_kv.shape[1:]),
            shape((all_rows, rows), F32),
        ),
        [HBM] * 6,
        [
            pltpu.VMEM((model, width), BF16),
            pltpu.VMEM(parents.shape, jnp.int32),
            pltpu.VMEM(long_parents.shape, jnp.int32),
            pltpu.SemaphoreType.DMA((requests + 5,)),
        ],
    )(xs, xl, w_hbm, kv_hbm, in_hbm(parents), in_hbm(long_parents))
    late = (w_qkv, short_kv, w_out, w_cross_q, enc_kv)
    late, queries = lax.optimization_barrier((late, queries))
    w_qkv, short_kv, w_out, w_cross_q, enc_kv = late
    long_pay = call(
        long_kernel, "long", shape((rows, pay)), [VMEM] * 3, flops=8 * 10**9
    )(queries, cache, jnp.broadcast_to(long_len.reshape(1, 1), (1, LANES)))
    got = [seq_pair(long_pay, k) for k in range(1, seqs)]
    other_kv = lax.ppermute(enc_kv, "req", [(i, i ^ 1) for i in range(reqs)])

    attn, draft, stats = call(
        attend_kernel,
        "attend",
        (shape((short_rows, width)), shape((rows, width), F32), shape((rows, LANES))),
        [VMEM] * 5 + [HBM],
        [pltpu.SMEM(short_len.shape, jnp.int32), pltpu.SemaphoreType.DMA((1,))],
        flops=4 * 10**9,
    )(queries, inputs, w_qkv, short_kv, tree, in_hbm(short_len))
    got, attn = lax.optimization_barrier((got, attn))
    partial = call(
        functools.partial(output_kernel, seqs - 1),
        "output",
        shape((all_rows, model)),
        [VMEM] * (4 + seqs),
        [pltpu.VMEM((all_rows, width), BF16), pltpu.VMEM((seqs, rows, pay), BF16)],
    )(attn, draft, stats, w_out, long_pay, *got)

    entries = seqs * requests + 1
    dys = tuple(range(pairs))
    docs, _ = lax.optimization_barrier((doc_ids, partial))
    kvs = call(
        functools.partial(fetch_kernel, seqs, requests, dys),
        "fetch",
        tuple(shape((entries, 2, CORES * span, width)) for _ in dys),
        [SMEM] * 2 + [HBM] * 2,
        [pltpu.SemaphoreType.DMA((pairs, entries, 2))],
        flops=4 * 10**9,
    )(docs, long_doc, in_hbm(enc_kv), other_kv)
    swapped, kvs = lax.optimization_barrier((tp_swap(partial), kvs))
    hidden_one, q_all, q_short = call(
        query_kernel,
        "query",
        (shape((all_rows, model)), shape((all_rows, width)), shape((short_rows, width))),
        [VMEM] * 4,
    )(inputs, partial, swapped, w_cross_q)

    pay_rows = all_rows + rows * LANES // width
    block = shape((pay_rows, width))
    groups = requests + 1
    half = seqs // 2
    odds, evens = list(range(1, seqs, 2)), list(range(2, seqs, 2))

    def near(kv, q):
        return call(
            functools.partial(near_kernel, requests),
            "near",
            (block, shape((rows, width)), shape((rows, LANES), F32)),
            [VMEM] * 2,
            flops=10**9,
        )(kv, q)

    def row(stacked, single, kv, long_o, long_stats, q):
        stack = [shape((len(stacked), pay_rows, width))] if stacked else []
        return call(
            functools.partial(row_kernel, requests, stacked, single),
            "row",
            stack + [block] * len(single),
            [VMEM] * 4,
            flops=10**9,
        )(kv, long_o, long_stats, q)

    def joined(skip, odd, even):
        return call(
            functools.partial(join_kernel, groups, skip),
            "join",
            [block] * len(even),
            [VMEM] * (1 + len(even)),
            [pltpu.VMEM((2, pay_rows, width), BF16)],
        )(odd, *even)

    shifted = [seq_pair(q_short, k) for k in range(1, seqs)]
    far_all = [yz_move(q_all, dy, 0) for dy in dys[1:]]
    zero, *long_part = near(kvs[0], q_all)
    shifted, zero = lax.optimization_barrier((shifted, zero))
    own_q = jnp.concatenate(shifted)
    far_q = [yz_move(own_q, dy, 0) for dy in dys[1:]]
    (odd,) = row(odds, [], kvs[0], *long_part, own_q)
    got = seq_pair(odd, 1)
    even = row([], evens, kvs[0], *long_part, own_q)
    ins = [zero, got]
    waiting = [(0, 1, got, even)]
    for dy in dys[1:]:
        q, even = lax.optimization_barrier((far_all[dy - 1], even))
        zero, *long_part = near(kvs[dy], q)
        ins.append(yz_move(zero, -dy, 0))
        q, _ = lax.optimization_barrier((far_q[dy - 1], zero))
        odd, one = row(odds[1:], odds[:1], kvs[dy], *long_part, q)
        got = seq_pair(odd, 1)
        ins.append(yz_move(one, -dy, 1))
        even = row([], evens, kvs[dy], *long_part, q)
        waiting.append((dy, 0, got, even))
    final = []
    for at, (dy, skip, got, even) in enumerate(waiting):
        final += ins[2 * at : 2 * at + 2]
        for e, x in zip(evens, joined(skip, got, even)):
            final.append(yz_move(x, -dy, e))
    partial = call(
        functools.partial(merge_kernel, dys, seqs, groups),
        "merge",
        shape((all_rows, model)),
        [VMEM] * (1 + len(final)),
        [
            pltpu.VMEM((pairs * half, pay_rows, width), BF16),
            pltpu.VMEM((2, pay_rows, width), BF16),
            pltpu.VMEM((all_rows, width), BF16),
        ],
    )(w_cross_out, *final)

    hidden_two, partial = call(
        ffn_kernel, "ffn", (shape((all_rows, model)),) * 2, [VMEM] * 5
    )(hidden_one, partial, tp_swap(partial), w_up, w_down)

    return call(
        final_kernel,
        "final",
        (shape((requests, rows, model)), shape((1, rows, model))),
        [VMEM] * 3,
    )(hidden_two, partial, tp_swap(partial))


def solution(mesh):
    in_specs = (
        P(("req", "seq"), None, None),
        P("req", None, None),
        P(("req", "seq"), None),
        P("req", None),
        P(("req", "seq")),
        P("req"),
        P(),
        P(),
        P(("req", "seq"), None, None, "tp"),
        P("req", None, "seq", "tp"),
        P(None, None, ("req", "seq"), "tp"),
        P(None, None, "tp"),
        P("tp", None),
        P(None, "tp"),
        P("tp", None),
        P(None, "tp"),
        P("tp", None),
    )
    out_specs = (P(("req", "seq"), None, None), P("req", None, None))
    return jax.shard_map(local, mesh=mesh, in_specs=in_specs, out_specs=out_specs, check_vma=False)
```

```python
import functools

import jax
import jax.numpy as jnp
from jax import lax
from jax.experimental import pallas as pl
from jax.experimental.pallas import tpu as pltpu
from jax.sharding import PartitionSpec as P

HD = 64
LANES = 128
CORES = 2
PIECES = 3
SLOTS = 4
CHUNK = 1024
OWN = 10**6
FAR = 10**10
MASKED = -1e30
EPS = 1e-05
F32 = jnp.float32
BF16 = jnp.bfloat16
VMEM = pl.BlockSpec(memory_space=pltpu.VMEM)
SMEM = pl.BlockSpec(memory_space=pltpu.SMEM)
HBM = pl.BlockSpec(memory_space=pltpu.HBM)


def iota(shape, axis):
    return lax.broadcasted_iota(jnp.int32, shape, axis)


def dot(a, b):
    return lax.dot_general(a, b, (((1,), (0,)), ((), ())), preferred_element_type=F32)


def dot_t(a, b):
    return lax.dot_general(a, b, (((1,), (1,)), ((), ())), preferred_element_type=F32)


def normalize(v):
    centered = v - jnp.mean(v, axis=-1, keepdims=True)
    return centered * lax.rsqrt(jnp.mean(centered * centered, axis=-1, keepdims=True) + EPS)


def halves(rows, dtype):
    low = (iota((rows, LANES), 1) < HD).astype(F32)
    return low.astype(dtype), (1.0 - low).astype(dtype)


def scores_of(q, k):
    rows, width = q.shape
    low, high = (half * HD ** (-0.5) for half in halves(rows, BF16))
    parts = []
    for at in range(0, width, LANES):
        tile = q[:, at : at + LANES]
        pair = jnp.concatenate([tile * low, tile * high], axis=0)
        parts.append(dot_t(pair, k[:, at : at + LANES]))
    return jnp.concatenate(parts, axis=0)


def sums_of(p):
    return dot(p, jnp.ones((p.shape[1], LANES), BF16))


def values_of(terms, total):
    width = terms[0][1].shape[1]
    rows = total.shape[0] * HD // width
    low = iota((rows, LANES), 1) < HD
    parts = []
    for at in range(0, width, LANES):
        row = at // HD * rows
        mid, end = row + rows, row + 2 * rows
        o = sum(dot(p[row:end], v[:, at : at + LANES]) for p, v in terms)
        o = jnp.where(low, o[:rows], o[rows:])
        parts.append(o / jnp.where(low, total[row:mid], total[mid:end]))
    return jnp.concatenate(parts, axis=1)


def spread(columns, heads):
    rows = columns.shape[0] // heads
    lane = iota((rows, LANES), 1) % heads
    out = jnp.zeros((rows, LANES), F32)
    for h in range(heads):
        out = jnp.where(lane == h, columns[h * rows : (h + 1) * rows], out)
    return out


def pack_stats(lse, heads, group=None):
    place = iota(lse.shape, 1) // heads
    if group is None:
        group, place = 0, place % SLOTS
    high = lse.astype(BF16).astype(F32)
    rest = lse - high
    mid = rest.astype(BF16).astype(F32)
    low = (rest - mid).astype(BF16).astype(F32)
    base = group * SLOTS
    packed = jnp.where(place == base, high, 0.0)
    packed = jnp.where(place == base + 1, mid, packed)
    return jnp.where(place == base + 2, low, packed)


def piece_hot(heads, group, shape, per_head):
    lane = iota(shape, 0)
    place = lane // heads - group * SLOTS
    hot = jnp.logical_and(lane % heads == per_head, place >= 0)
    return jnp.logical_and(hot, place < PIECES).astype(F32).astype(BF16)


def expand_stats(stats, heads, group=0):
    shape = (LANES, heads * HD)
    return dot(stats, piece_hot(heads, group, shape, iota(shape, 1) // HD))


def respread(stats, heads):
    shape = (LANES, LANES)
    return dot(stats, piece_hot(heads, 0, shape, iota(shape, 1) % heads))


def softmax_part(s, v, heads, allowed=None):
    if allowed is not None:
        s = jnp.where(allowed, s, MASKED)
    m = jnp.max(s, axis=-1, keepdims=True)
    p = jnp.exp(s - m)
    if allowed is not None:
        p = jnp.where(allowed, p, 0.0)
    p = p.astype(BF16)
    l = jnp.maximum(sums_of(p), 1e-30)
    return values_of([(p, v)], l), spread(m, heads) + jnp.log(spread(l, heads))


def merge(values, scores):
    top = functools.reduce(jnp.maximum, scores)
    total = acc = None
    for value, score in zip(values, scores):
        w = jnp.exp(score - top)
        total = w if total is None else total + w
        acc = w * value if acc is None else acc + w * value
    return acc / total


def ancestors(parents, rows):
    nodes = parents.shape[1]
    node_j = iota((nodes, nodes), 0)
    node_i = iota((nodes, nodes), 1)
    target = parents + node_i // rows * rows
    hot = jnp.logical_and(target == node_j, node_i % rows > 0).astype(F32)
    closure = (node_i == node_j).astype(F32) + hot
    reach = 1
    while reach < rows:
        b = closure.astype(BF16)
        closure = jnp.minimum(dot(b, b), 1.0)
        reach *= 2
    shape = (nodes, rows)
    place = (iota(shape, 0) % rows == iota(shape, 1)).astype(F32)
    return lax.dot_general(
        closure.astype(BF16),
        place.astype(BF16),
        (((0,), (0,)), ((), ())),
        preferred_element_type=F32,
    )


def first_kernel(
    xs_hbm, xl_hbm, w_hbm, kv_hbm, ps_hbm, lp_hbm, q_ref, x_ref, kv_ref, tree_ref, w, ps, lp, sems
):
    requests, rows, model = xs_hbm.shape
    short_rows = requests * rows
    moves = [(ps_hbm, ps), (lp_hbm, lp)]
    moves += [(xs_hbm.at[j], x_ref.at[pl.ds(j * rows, rows)]) for j in range(requests)]
    moves += [(xl_hbm.at[0], x_ref.at[pl.ds(short_rows, rows)]), (w_hbm.at[0], w)]
    moves += [(kv_hbm.at[0], kv_ref)]
    copies = [pltpu.make_async_copy(a, b, sems.at[i]) for i, (a, b) in enumerate(moves)]
    for copy in copies:
        copy.start()
    for copy in copies[:2]:
        copy.wait()
    parents = [ps[j : j + 1, :] for j in range(requests)] + [lp[...]]
    tree_ref[...] = ancestors(jnp.concatenate(parents, axis=1), rows)
    for copy in copies[2:-1]:
        copy.wait()
    q_ref[...] = dot(x_ref[...], w[...]).astype(BF16)
    copies[-1].wait()


def long_kernel(q_ref, kv_ref, len_ref, pay_ref):
    rows = pay_ref.shape[0]
    width = q_ref.shape[1]
    heads = width // HD
    span = kv_ref.shape[1]
    allowed = iota((1, span), 1) + lax.axis_index("seq") * span < len_ref[:, :1]
    s = scores_of(q_ref[q_ref.shape[0] - rows :, :], kv_ref[0])
    o, lse = softmax_part(s, kv_ref[1], heads, allowed)
    pay_ref[:, :width] = o.astype(BF16)
    pay_ref[:, width:] = pack_stats(lse, heads, 0).astype(BF16)


def short_attend(q, k, v, cache_k, cache_v, allowed, tree, heads):
    allowed_d = jnp.concatenate([tree] * heads, axis=0) > 0.5
    s = jnp.where(allowed, scores_of(q, cache_k), MASKED)
    d = jnp.where(allowed_d, scores_of(q, k), MASKED)
    m = jnp.maximum(jnp.max(s, axis=-1, keepdims=True), jnp.max(d, axis=-1, keepdims=True))
    p = jnp.exp(s - m).astype(BF16)
    pd = jnp.exp(d - m).astype(BF16)
    return values_of([(p, cache_v), (pd, v)], sums_of(p) + sums_of(pd)).astype(BF16)


def attend_kernel(
    q_ref, x_ref, w_ref, skv_ref, tree_ref, sl_hbm, attn_ref, draft_ref, stat_ref, sl, sem
):
    requests = skv_ref.shape[0]
    rows = tree_ref.shape[1]
    copy = pltpu.make_async_copy(sl_hbm, sl, sem.at[0])
    copy.start()
    heads = q_ref.shape[1] // HD
    span = skv_ref.shape[2]
    x = x_ref[...]
    k = dot(x, w_ref[1]).astype(BF16)
    v = dot(x, w_ref[2]).astype(BF16)
    row = requests * rows
    allowed = jnp.concatenate([tree_ref[row:, :]] * heads, axis=0) > 0.5
    s = scores_of(q_ref[row:, :], k[row:])
    o, lse = softmax_part(s, v[row:], heads, allowed)
    draft_ref[...] = o
    stat_ref[...] = pack_stats(lse, heads, 0).astype(BF16)
    copy.wait()
    for j in range(requests):
        part = slice(j * rows, (j + 1) * rows)
        attn_ref[part, :] = short_attend(
            q_ref[part, :], k[part], v[part], skv_ref[j, 0], skv_ref[j, 1],
            iota((1, span), 1) < sl[j], tree_ref[part, :], heads,
        )


def output_kernel(hops, attn_ref, draft_ref, stat_ref, wo_ref, *rest):
    pay_refs, (out_ref, attn, pays) = rest[: hops + 1], rest[hops + 1 :]
    short_rows, width = attn_ref.shape
    heads = width // HD
    zed = lax.axis_index("seq")
    for hop, ref in enumerate(pay_refs):
        pays[zed ^ hop] = ref[...]
    values = [draft_ref[...]] + [pays[z, :, :width].astype(F32) for z in range(hops + 1)]
    scores = [expand_stats(stat_ref[...], heads)] + [
        expand_stats(pays[z, :, width:], heads) for z in range(hops + 1)
    ]
    attn[:short_rows, :] = attn_ref[...]
    attn[short_rows:, :] = merge(values, scores).astype(BF16)
    out_ref[...] = dot(attn[...], wo_ref[...]).astype(BF16)


def query_kernel(x_ref, a_ref, b_ref, w_ref, h_ref, q_ref, qs_ref):
    short_rows = qs_ref.shape[0]
    x = x_ref[...].astype(F32)
    h = normalize(x + (a_ref[...].astype(F32) + b_ref[...].astype(F32))).astype(BF16)
    h_ref[...] = h
    q = dot(h, w_ref[...]).astype(BF16)
    q_ref[...] = q
    qs_ref[...] = q[:short_rows]


def fetch_kernel(seqs, requests, dys, doc_ref, long_ref, own_ref, other_ref, *rest):
    outs, sems = rest[: len(dys)], rest[len(dys)]
    span = own_ref.shape[2]
    short_total = seqs * requests
    zed = lax.axis_index("seq")
    req = lax.axis_index("req")
    pairs = lax.axis_size("req") // CORES
    for at, dy in enumerate(dys):
        group = lax.rem(req // CORES - dy + pairs, pairs) * CORES + lax.rem(req, CORES)
        kv = outs[at]
        copies = []
        for e in range(short_total + 1):
            if e == short_total:
                doc = long_ref[group]
            else:
                place = zed ^ (e // requests)
                doc = doc_ref[(group * seqs + place) * requests + e % requests]
            for half, ref in enumerate((own_ref, other_ref)):
                copies.append(
                    pltpu.make_async_copy(
                        ref.at[:, doc],
                        kv.at[e, :, pl.ds(half * span, span)],
                        sems.at[at, e, half],
                    )
                )
                copies[-1].start()
        if at == 0:
            first = copies
        else:
            first = first + copies
    for copy in first:
        copy.wait()


def document_part(kv_ref, e, q, heads, group):
    o, lse = softmax_part(scores_of(q, kv_ref[e, 0]), kv_ref[e, 1], heads)
    return o.astype(BF16), pack_stats(lse, heads, group)


def fill(pay_ref, parts, long_o, long_stats):
    rows = long_o.shape[0]
    for j, (o, more) in enumerate(parts):
        pay_ref[j * rows : (j + 1) * rows, :] = o
        long_stats = long_stats + more
    end = (len(parts) + 1) * rows
    pay_ref[end - rows : end, :] = long_o
    write_stats(pay_ref, end, long_stats)


def write_stats(pay_ref, row, stats):
    for at in range(0, stats.shape[0], 8):
        lanes = slice(at // 8 * LANES, (at // 8 + 1) * LANES)
        pay_ref[row : row + 8, lanes] = stats[at : at + 8].astype(BF16)


def read_stats(block):
    block = block.astype(F32)
    tiles = [block[:, at : at + LANES] for at in range(0, block.shape[1], LANES)]
    return jnp.concatenate(tiles, axis=0).astype(BF16)


def near_kernel(requests, kv_ref, q_ref, pay_ref, o_ref, stat_ref):
    rows, width = o_ref.shape
    heads = width // HD
    last = q_ref.shape[0] - rows
    o, stats = document_part(kv_ref, kv_ref.shape[0] - 1, q_ref[last:, :], heads, requests)
    o_ref[...] = o
    stat_ref[...] = stats
    parts = [
        document_part(kv_ref, j, q_ref[j * rows : (j + 1) * rows, :], heads, j)
        for j in range(requests)
    ]
    fill(pay_ref, parts, o, stats)


def row_kernel(requests, stacked, single, kv_ref, o_ref, stat_ref, q_ref, *outs):
    ks = stacked + single
    rows, width = o_ref.shape
    heads = width // HD
    targets = [outs[0].at[i] for i in range(len(stacked))]
    targets += outs[1 if stacked else 0 :]
    for k, target in zip(ks, targets):
        parts = []
        for j in range(requests):
            row = ((k - 1) * requests + j) * rows
            q = q_ref[row : row + rows, :]
            parts.append(document_part(kv_ref, k * requests + j, q, heads, j))
        fill(target, parts, o_ref[...], stat_ref[...])


def join(two, out, groups, heads):
    rows, width = out.shape
    step = rows * width // (groups * width + LANES)
    end = groups * step
    lane, other = (iota((LANES, LANES), axis) for axis in range(2))
    slots = heads * SLOTS
    hot = jnp.logical_and(lane % heads == other % heads, lane // slots == other // slots)
    hot = jnp.logical_and(hot, lane // heads % SLOTS < PIECES).astype(F32).astype(BF16)
    stats = [read_stats(two[i, end:, :]) for i in range(2)]
    for group in range(groups):
        part = slice(group * step, (group + 1) * step)
        scores = [expand_stats(x, heads, group) for x in stats]
        out[part, :] = merge([two[i, part, :].astype(F32) for i in range(2)], scores).astype(BF16)
    left, right = (dot(x, hot) for x in stats)
    top = jnp.maximum(left, right)
    lse = top + jnp.log(jnp.exp(left - top) + jnp.exp(right - top))
    write_stats(out, end, pack_stats(lse, heads))


def join_kernel(groups, skip, odd_ref, *rest):
    count = len(rest) // 2
    two = rest[-1]
    heads = two.shape[2] // HD
    odd_z = lax.axis_index("seq") & 1
    for e in range(count):
        two[odd_z] = rest[e][...]
        two[1 - odd_z] = odd_ref[skip + e]
        join(two, rest[count + e], groups, heads)


def merge_kernel(dys, seqs, groups, w_ref, *rest):
    half = seqs // 2
    ins, (out_ref, pays, two, cross) = rest[:-4], rest[-4:]
    all_rows, width = cross.shape
    heads = width // HD
    pairs = lax.axis_size("req") // CORES
    yed = lax.axis_index("req") // CORES
    zed = lax.axis_index("seq")
    odd_z = zed & 1
    for dy in dys:
        base = lax.rem(yed + dy, pairs) * half
        if dy:
            zero, one, *far = ins[: half + 1]
            two[odd_z] = zero[...]
            two[1 - odd_z] = one[...]
            join(two, pays.at[base + zed // 2], groups, heads)
        else:
            zero, *far = ins[:half]
            pays[base + zed // 2] = zero[...]
        ins = ins[half + 1 if dy else half :]
        for e, ref in enumerate(far, 1):
            pays[base + (zed ^ (2 * e)) // 2] = ref[...]
    total = len(dys) * half
    stats = [read_stats(pays[s, all_rows:, :]) for s in range(total)]
    step = all_rows // groups
    for group in range(groups):
        part = slice(group * step, (group + 1) * step)
        values = [pays[s, part, :].astype(F32) for s in range(total)]
        scores = [expand_stats(stats[s], heads, group) for s in range(total)]
        cross[part, :] = merge(values, scores).astype(BF16)
    out_ref[...] = dot(cross[...], w_ref[...]).astype(BF16)


def gelu(x):
    return 0.5 * x * (1.0 + lax.erf(x * 0.5**0.5))


def ffn_kernel(h_ref, a_ref, b_ref, up_ref, down_ref, h2_ref, out_ref):
    total = h_ref[...].astype(F32) + (a_ref[...].astype(F32) + b_ref[...].astype(F32))
    h2 = normalize(total).astype(BF16)
    h2_ref[...] = h2
    acc = None
    for at in range(0, up_ref.shape[1], CHUNK):
        act = gelu(dot(h2, up_ref[:, at : at + CHUNK])).astype(BF16)
        part = dot(act, down_ref[at : at + CHUNK, :])
        acc = part if acc is None else acc + part
    out_ref[...] = acc.astype(BF16)


def final_kernel(h_ref, a_ref, b_ref, ys_ref, yl_ref):
    total = h_ref[...].astype(F32) + (a_ref[...].astype(F32) + b_ref[...].astype(F32))
    y = normalize(total).astype(BF16)
    short_rows = ys_ref.shape[0] * ys_ref.shape[1]
    ys_ref[...] = y[:short_rows].reshape(ys_ref.shape)
    yl_ref[0] = y[short_rows:]


def call(kernel, name, out, ins, scratch=(), flops=10**8, moved=10**6, grant=16 << 20):
    many = isinstance(out, (tuple, list))
    return pl.pallas_call(
        kernel,
        out_shape=out,
        in_specs=ins,
        out_specs=[VMEM] * len(out) if many else VMEM,
        scratch_shapes=list(scratch),
        name=name,
        cost_estimate=pl.CostEstimate(flops=flops, bytes_accessed=moved, transcendentals=0),
        compiler_params=pltpu.CompilerParams(vmem_limit_bytes=grant),
    )


def in_hbm(x):
    return pltpu.with_memory_space_constraint(x, pltpu.HBM)


def shape(dims, dtype=BF16):
    return jax.ShapeDtypeStruct(dims, dtype)


def local(
    x_short,
    x_long,
    parents,
    long_parents,
    short_len,
    long_len,
    doc_ids,
    long_doc,
    short_kv,
    long_kv,
    enc_kv,
    w_qkv,
    w_out,
    w_cross_q,
    w_cross_out,
    w_up,
    w_down,
):
    requests, rows, model = x_short.shape
    width = w_qkv.shape[2]
    heads = width // HD
    short_rows = requests * rows
    all_rows = short_rows + rows
    seqs = lax.axis_size("seq")
    reqs = lax.axis_size("req")
    tps = lax.axis_size("tp")
    pairs = reqs // CORES
    pay = width + LANES
    span = enc_kv.shape[2]
    both = ("req", "seq")

    def seq_pair(x, k):
        return lax.ppermute(x, "seq", [(i, i ^ k) for i in range(seqs)])

    def yz_move(x, dy, dz):
        perm = []
        for y in range(pairs):
            for c in range(CORES):
                for z in range(seqs):
                    to = ((y + dy) % pairs * CORES + c) * seqs + (z ^ dz)
                    perm.append(((y * CORES + c) * seqs + z, to))
        return lax.ppermute(x, both, perm)

    def tp_swap(x):
        return lax.ppermute(x, "tp", [(i, (i + 1) % tps) for i in range(tps)])

    xs, xl, w_hbm, kv_hbm = map(in_hbm, (x_short, x_long, w_qkv, long_kv))
    queries, inputs, cache, tree = call(
        first_kernel,
        "first",
        (
            shape((all_rows, width)),
            shape((all_rows, model)),
            shape(long_kv.shape[1:]),
            shape((all_rows, rows), F32),
        ),
        [HBM] * 6,
        [
            pltpu.VMEM((model, width), BF16),
            pltpu.VMEM(parents.shape, jnp.int32),
            pltpu.VMEM(long_parents.shape, jnp.int32),
            pltpu.SemaphoreType.DMA((requests + 5,)),
        ],
    )(xs, xl, w_hbm, kv_hbm, in_hbm(parents), in_hbm(long_parents))
    late = (w_qkv, short_kv, w_out, w_cross_q, enc_kv)
    late, queries = lax.optimization_barrier((late, queries))
    w_qkv, short_kv, w_out, w_cross_q, enc_kv = late
    long_pay = call(
        long_kernel, "long", shape((rows, pay)), [VMEM] * 3, flops=8 * 10**9
    )(queries, cache, jnp.broadcast_to(long_len.reshape(1, 1), (1, LANES)))
    got = [seq_pair(long_pay, k) for k in range(1, seqs)]
    other_kv = lax.ppermute(enc_kv, "req", [(i, i ^ 1) for i in range(reqs)])

    attn, draft, stats = call(
        attend_kernel,
        "attend",
        (shape((short_rows, width)), shape((rows, width), F32), shape((rows, LANES))),
        [VMEM] * 5 + [HBM],
        [pltpu.SMEM(short_len.shape, jnp.int32), pltpu.SemaphoreType.DMA((1,))],
        flops=4 * 10**9,
    )(queries, inputs, w_qkv, short_kv, tree, in_hbm(short_len))
    got, attn = lax.optimization_barrier((got, attn))
    partial = call(
        functools.partial(output_kernel, seqs - 1),
        "output",
        shape((all_rows, model)),
        [VMEM] * (4 + seqs),
        [pltpu.VMEM((all_rows, width), BF16), pltpu.VMEM((seqs, rows, pay), BF16)],
    )(attn, draft, stats, w_out, long_pay, *got)

    entries = seqs * requests + 1
    dys = tuple(range(pairs))
    docs, _ = lax.optimization_barrier((doc_ids, partial))
    kvs = call(
        functools.partial(fetch_kernel, seqs, requests, dys),
        "fetch",
        tuple(shape((entries, 2, CORES * span, width)) for _ in dys),
        [SMEM] * 2 + [HBM] * 2,
        [pltpu.SemaphoreType.DMA((pairs, entries, 2))],
        flops=4 * 10**9,
    )(docs, long_doc, in_hbm(enc_kv), other_kv)
    swapped, kvs = lax.optimization_barrier((tp_swap(partial), kvs))
    hidden_one, q_all, q_short = call(
        query_kernel,
        "query",
        (shape((all_rows, model)), shape((all_rows, width)), shape((short_rows, width))),
        [VMEM] * 4,
    )(inputs, partial, swapped, w_cross_q)

    pay_rows = all_rows + rows * LANES // width
    block = shape((pay_rows, width))
    groups = requests + 1
    half = seqs // 2
    odds, evens = list(range(1, seqs, 2)), list(range(2, seqs, 2))

    def near(kv, q, flops):
        return call(
            functools.partial(near_kernel, requests),
            "near",
            (block, shape((rows, width)), shape((rows, LANES), F32)),
            [VMEM] * 2,
            flops=flops,
        )(kv, q)

    def row(stacked, single, kv, long_o, long_stats, q, flops):
        stack = [shape((len(stacked), pay_rows, width))] if stacked else []
        return call(
            functools.partial(row_kernel, requests, stacked, single),
            "row",
            stack + [block] * len(single),
            [VMEM] * 4,
            flops=flops,
        )(kv, long_o, long_stats, q)

    def joined(skip, odd, even, flops):
        return call(
            functools.partial(join_kernel, groups, skip),
            "join",
            [block] * len(even),
            [VMEM] * (1 + len(even)),
            [pltpu.VMEM((2, pay_rows, width), BF16)],
            flops=flops,
        )(odd, *even)

    far_all = [yz_move(q_all, dy, 0) for dy in dys[1:]]
    shifted = [seq_pair(q_short, k) for k in range(1, seqs)]
    zero, *long_part = near(kvs[0], q_all, 10**9)
    shifted, zero = lax.optimization_barrier((shifted, zero))
    own_q = jnp.concatenate(shifted)
    far_q = [yz_move(own_q, dy, 0) for dy in dys[1:]]
    (odd,) = row(odds, [], kvs[0], *long_part, own_q, OWN)
    got = seq_pair(odd, 1)
    even = row([], evens, kvs[0], *long_part, own_q, OWN)
    first, *rest = joined(0, got, [zero, *even], OWN)
    own = [first] + [yz_move(x, 0, e) for e, x in zip(evens, rest)]
    final = []
    for dy in dys[1:]:
        q, even = lax.optimization_barrier((far_all[dy - 1], even))
        zero, *long_part = near(kvs[dy], q, FAR)
        qs, _ = lax.optimization_barrier((far_q[dy - 1], zero))
        odd, one = row(odds[1:], odds[:1], kvs[dy], *long_part, qs, FAR)
        got = seq_pair(odd, 1)
        even = row([], evens, kvs[dy], *long_part, qs, FAR)
        rest = joined(0, got, even, FAR)
        final += [yz_move(zero, -dy, 0), yz_move(one, -dy, 1)]
        final += [yz_move(x, -dy, e) for e, x in zip(evens, rest)]
    final = own + final
    partial = call(
        functools.partial(merge_kernel, dys, seqs, groups),
        "merge",
        shape((all_rows, model)),
        [VMEM] * (1 + len(final)),
        [
            pltpu.VMEM((pairs * half, pay_rows, width), BF16),
            pltpu.VMEM((2, pay_rows, width), BF16),
            pltpu.VMEM((all_rows, width), BF16),
        ],
    )(w_cross_out, *final)

    hidden_two, partial = call(
        ffn_kernel, "ffn", (shape((all_rows, model)),) * 2, [VMEM] * 5
    )(hidden_one, partial, tp_swap(partial), w_up, w_down)

    return call(
        final_kernel,
        "final",
        (shape((requests, rows, model)), shape((1, rows, model))),
        [VMEM] * 3,
    )(hidden_two, partial, tp_swap(partial))


def solution(mesh):
    in_specs = (
        P(("req", "seq"), None, None),
        P("req", None, None),
        P(("req", "seq"), None),
        P("req", None),
        P(("req", "seq")),
        P("req"),
        P(),
        P(),
        P(("req", "seq"), None, None, "tp"),
        P("req", None, "seq", "tp"),
        P(None, None, ("req", "seq"), "tp"),
        P(None, None, "tp"),
        P("tp", None),
        P(None, "tp"),
        P("tp", None),
        P(None, "tp"),
        P("tp", None),
    )
    out_specs = (P(("req", "seq"), None, None), P("req", None, None))
    return jax.shard_map(local, mesh=mesh, in_specs=in_specs, out_specs=out_specs, check_vma=False)
```

```python
import functools

import jax
import jax.numpy as jnp
from jax import lax
from jax.experimental import pallas as pl
from jax.experimental.pallas import tpu as pltpu
from jax.sharding import PartitionSpec as P

HD = 64
LANES = 128
CORES = 2
PIECES = 3
SLOTS = 4
CHUNK = 1024
OWN = 10**6
FAR = 10**10
MASKED = -1e30
EPS = 1e-05
F32 = jnp.float32
BF16 = jnp.bfloat16
VMEM = pl.BlockSpec(memory_space=pltpu.VMEM)
SMEM = pl.BlockSpec(memory_space=pltpu.SMEM)
HBM = pl.BlockSpec(memory_space=pltpu.HBM)


def iota(shape, axis):
    return lax.broadcasted_iota(jnp.int32, shape, axis)


def dot(a, b):
    return lax.dot_general(a, b, (((1,), (0,)), ((), ())), preferred_element_type=F32)


def dot_t(a, b):
    return lax.dot_general(a, b, (((1,), (1,)), ((), ())), preferred_element_type=F32)


def normalize(v):
    centered = v - jnp.mean(v, axis=-1, keepdims=True)
    return centered * lax.rsqrt(jnp.mean(centered * centered, axis=-1, keepdims=True) + EPS)


def halves(rows, dtype):
    low = (iota((rows, LANES), 1) < HD).astype(F32)
    return low.astype(dtype), (1.0 - low).astype(dtype)


def scores_of(q, k):
    rows, width = q.shape
    low, high = (half * HD ** (-0.5) for half in halves(rows, BF16))
    parts = []
    for at in range(0, width, LANES):
        tile = q[:, at : at + LANES]
        pair = jnp.concatenate([tile * low, tile * high], axis=0)
        parts.append(dot_t(pair, k[:, at : at + LANES]))
    return jnp.concatenate(parts, axis=0)


def sums_of(p):
    return dot(p, jnp.ones((p.shape[1], LANES), BF16))


def values_of(terms, total):
    width = terms[0][1].shape[1]
    rows = total.shape[0] * HD // width
    low = iota((rows, LANES), 1) < HD
    parts = []
    for at in range(0, width, LANES):
        row = at // HD * rows
        mid, end = row + rows, row + 2 * rows
        o = sum(dot(p[row:end], v[:, at : at + LANES]) for p, v in terms)
        o = jnp.where(low, o[:rows], o[rows:])
        parts.append(o / jnp.where(low, total[row:mid], total[mid:end]))
    return jnp.concatenate(parts, axis=1)


def spread(columns, heads):
    rows = columns.shape[0] // heads
    lane = iota((rows, LANES), 1) % heads
    out = jnp.zeros((rows, LANES), F32)
    for h in range(heads):
        out = jnp.where(lane == h, columns[h * rows : (h + 1) * rows], out)
    return out


def pack_stats(lse, heads, group=None):
    place = iota(lse.shape, 1) // heads
    if group is None:
        group, place = 0, place % SLOTS
    high = lse.astype(BF16).astype(F32)
    rest = lse - high
    mid = rest.astype(BF16).astype(F32)
    low = (rest - mid).astype(BF16).astype(F32)
    base = group * SLOTS
    packed = jnp.where(place == base, high, 0.0)
    packed = jnp.where(place == base + 1, mid, packed)
    return jnp.where(place == base + 2, low, packed)


def piece_hot(heads, group, shape, per_head):
    lane = iota(shape, 0)
    place = lane // heads - group * SLOTS
    hot = jnp.logical_and(lane % heads == per_head, place >= 0)
    return jnp.logical_and(hot, place < PIECES).astype(F32).astype(BF16)


def expand_stats(stats, heads, group=0):
    shape = (LANES, heads * HD)
    return dot(stats, piece_hot(heads, group, shape, iota(shape, 1) // HD))


def respread(stats, heads):
    shape = (LANES, LANES)
    return dot(stats, piece_hot(heads, 0, shape, iota(shape, 1) % heads))


def softmax_part(s, v, heads, allowed=None):
    if allowed is not None:
        s = jnp.where(allowed, s, MASKED)
    m = jnp.max(s, axis=-1, keepdims=True)
    p = jnp.exp(s - m)
    if allowed is not None:
        p = jnp.where(allowed, p, 0.0)
    p = p.astype(BF16)
    l = jnp.maximum(sums_of(p), 1e-30)
    return values_of([(p, v)], l), spread(m, heads) + jnp.log(spread(l, heads))


def merge(values, scores):
    top = functools.reduce(jnp.maximum, scores)
    total = acc = None
    for value, score in zip(values, scores):
        w = jnp.exp(score - top)
        total = w if total is None else total + w
        acc = w * value if acc is None else acc + w * value
    return acc / total


def ancestors(parents, rows):
    nodes = parents.shape[1]
    node_j = iota((nodes, nodes), 0)
    node_i = iota((nodes, nodes), 1)
    target = parents + node_i // rows * rows
    hot = jnp.logical_and(target == node_j, node_i % rows > 0).astype(F32)
    closure = (node_i == node_j).astype(F32) + hot
    reach = 1
    while reach < rows:
        b = closure.astype(BF16)
        closure = jnp.minimum(dot(b, b), 1.0)
        reach *= 2
    shape = (nodes, rows)
    place = (iota(shape, 0) % rows == iota(shape, 1)).astype(F32)
    return lax.dot_general(
        closure.astype(BF16),
        place.astype(BF16),
        (((0,), (0,)), ((), ())),
        preferred_element_type=F32,
    )


def first_kernel(
    xs_hbm, xl_hbm, w_hbm, kv_hbm, ps_hbm, lp_hbm, q_ref, x_ref, kv_ref, tree_ref, w, ps, lp, sems
):
    requests, rows, model = xs_hbm.shape
    short_rows = requests * rows
    moves = [(ps_hbm, ps), (lp_hbm, lp)]
    moves += [(xs_hbm.at[j], x_ref.at[pl.ds(j * rows, rows)]) for j in range(requests)]
    moves += [(xl_hbm.at[0], x_ref.at[pl.ds(short_rows, rows)]), (w_hbm.at[0], w)]
    moves += [(kv_hbm.at[0], kv_ref)]
    copies = [pltpu.make_async_copy(a, b, sems.at[i]) for i, (a, b) in enumerate(moves)]
    for copy in copies:
        copy.start()
    for copy in copies[:2]:
        copy.wait()
    parents = [ps[j : j + 1, :] for j in range(requests)] + [lp[...]]
    tree_ref[...] = ancestors(jnp.concatenate(parents, axis=1), rows)
    for copy in copies[2:-1]:
        copy.wait()
    q_ref[...] = dot(x_ref[...], w[...]).astype(BF16)
    copies[-1].wait()


def long_kernel(q_ref, kv_ref, len_ref, pay_ref):
    rows = pay_ref.shape[0]
    width = q_ref.shape[1]
    heads = width // HD
    span = kv_ref.shape[1]
    allowed = iota((1, span), 1) + lax.axis_index("seq") * span < len_ref[:, :1]
    s = scores_of(q_ref[q_ref.shape[0] - rows :, :], kv_ref[0])
    o, lse = softmax_part(s, kv_ref[1], heads, allowed)
    pay_ref[:, :width] = o.astype(BF16)
    pay_ref[:, width:] = pack_stats(lse, heads, 0).astype(BF16)


def short_attend(q, k, v, cache_k, cache_v, allowed, tree, heads):
    allowed_d = jnp.concatenate([tree] * heads, axis=0) > 0.5
    s = jnp.where(allowed, scores_of(q, cache_k), MASKED)
    d = jnp.where(allowed_d, scores_of(q, k), MASKED)
    m = jnp.maximum(jnp.max(s, axis=-1, keepdims=True), jnp.max(d, axis=-1, keepdims=True))
    p = jnp.exp(s - m).astype(BF16)
    pd = jnp.exp(d - m).astype(BF16)
    return values_of([(p, cache_v), (pd, v)], sums_of(p) + sums_of(pd)).astype(BF16)


def attend_kernel(
    q_ref, x_ref, w_ref, skv_ref, tree_ref, sl_hbm, attn_ref, draft_ref, stat_ref, sl, sem
):
    requests = skv_ref.shape[0]
    rows = tree_ref.shape[1]
    copy = pltpu.make_async_copy(sl_hbm, sl, sem.at[0])
    copy.start()
    heads = q_ref.shape[1] // HD
    span = skv_ref.shape[2]
    x = x_ref[...]
    k = dot(x, w_ref[1]).astype(BF16)
    v = dot(x, w_ref[2]).astype(BF16)
    row = requests * rows
    allowed = jnp.concatenate([tree_ref[row:, :]] * heads, axis=0) > 0.5
    s = scores_of(q_ref[row:, :], k[row:])
    o, lse = softmax_part(s, v[row:], heads, allowed)
    draft_ref[...] = o
    stat_ref[...] = pack_stats(lse, heads, 0).astype(BF16)
    copy.wait()
    for j in range(requests):
        part = slice(j * rows, (j + 1) * rows)
        attn_ref[part, :] = short_attend(
            q_ref[part, :], k[part], v[part], skv_ref[j, 0], skv_ref[j, 1],
            iota((1, span), 1) < sl[j], tree_ref[part, :], heads,
        )


def output_kernel(hops, attn_ref, draft_ref, stat_ref, wo_ref, *rest):
    pay_refs, (out_ref, attn, pays) = rest[: hops + 1], rest[hops + 1 :]
    short_rows, width = attn_ref.shape
    heads = width // HD
    zed = lax.axis_index("seq")
    for hop, ref in enumerate(pay_refs):
        pays[zed ^ hop] = ref[...]
    values = [draft_ref[...]] + [pays[z, :, :width].astype(F32) for z in range(hops + 1)]
    scores = [expand_stats(stat_ref[...], heads)] + [
        expand_stats(pays[z, :, width:], heads) for z in range(hops + 1)
    ]
    attn[:short_rows, :] = attn_ref[...]
    attn[short_rows:, :] = merge(values, scores).astype(BF16)
    out_ref[...] = dot(attn[...], wo_ref[...]).astype(BF16)


def query_kernel(x_ref, a_ref, b_ref, w_ref, h_ref, q_ref, qs_ref):
    short_rows = qs_ref.shape[0]
    x = x_ref[...].astype(F32)
    h = normalize(x + (a_ref[...].astype(F32) + b_ref[...].astype(F32))).astype(BF16)
    h_ref[...] = h
    q = dot(h, w_ref[...]).astype(BF16)
    q_ref[...] = q
    qs_ref[...] = q[:short_rows]


def fetch_kernel(seqs, requests, dys, doc_ref, long_ref, own_ref, other_ref, *rest):
    outs, sems = rest[: len(dys)], rest[len(dys)]
    span = own_ref.shape[2]
    short_total = seqs * requests
    zed = lax.axis_index("seq")
    req = lax.axis_index("req")
    pairs = lax.axis_size("req") // CORES
    for at, dy in enumerate(dys):
        group = lax.rem(req // CORES - dy + pairs, pairs) * CORES + lax.rem(req, CORES)
        kv = outs[at]
        copies = []
        for e in range(short_total + 1):
            if e == short_total:
                doc = long_ref[group]
            else:
                place = zed ^ (e // requests)
                doc = doc_ref[(group * seqs + place) * requests + e % requests]
            for half, ref in enumerate((own_ref, other_ref)):
                copies.append(
                    pltpu.make_async_copy(
                        ref.at[:, doc],
                        kv.at[e, :, pl.ds(half * span, span)],
                        sems.at[at, e, half],
                    )
                )
                copies[-1].start()
        if at == 0:
            first = copies
        else:
            first = first + copies
    for copy in first:
        copy.wait()


def document_part(kv_ref, e, q, heads, group):
    o, lse = softmax_part(scores_of(q, kv_ref[e, 0]), kv_ref[e, 1], heads)
    return o.astype(BF16), pack_stats(lse, heads, group)


def fill(pay_ref, parts, long_o, long_stats):
    rows = long_o.shape[0]
    for j, (o, more) in enumerate(parts):
        pay_ref[j * rows : (j + 1) * rows, :] = o
        long_stats = long_stats + more
    end = (len(parts) + 1) * rows
    pay_ref[end - rows : end, :] = long_o
    write_stats(pay_ref, end, long_stats)


def write_stats(pay_ref, row, stats):
    for at in range(0, stats.shape[0], 8):
        lanes = slice(at // 8 * LANES, (at // 8 + 1) * LANES)
        pay_ref[row : row + 8, lanes] = stats[at : at + 8].astype(BF16)


def read_stats(block):
    block = block.astype(F32)
    tiles = [block[:, at : at + LANES] for at in range(0, block.shape[1], LANES)]
    return jnp.concatenate(tiles, axis=0).astype(BF16)


def near_kernel(requests, kv_ref, q_ref, pay_ref, o_ref, stat_ref):
    rows, width = o_ref.shape
    heads = width // HD
    last = q_ref.shape[0] - rows
    o, stats = document_part(kv_ref, kv_ref.shape[0] - 1, q_ref[last:, :], heads, requests)
    o_ref[...] = o
    stat_ref[...] = stats
    parts = [
        document_part(kv_ref, j, q_ref[j * rows : (j + 1) * rows, :], heads, j)
        for j in range(requests)
    ]
    fill(pay_ref, parts, o, stats)


def row_kernel(requests, stacked, single, kv_ref, o_ref, stat_ref, q_ref, *outs):
    ks = stacked + single
    rows, width = o_ref.shape
    heads = width // HD
    targets = [outs[0].at[i] for i in range(len(stacked))]
    targets += outs[1 if stacked else 0 :]
    for k, target in zip(ks, targets):
        parts = []
        for j in range(requests):
            row = ((k - 1) * requests + j) * rows
            q = q_ref[row : row + rows, :]
            parts.append(document_part(kv_ref, k * requests + j, q, heads, j))
        fill(target, parts, o_ref[...], stat_ref[...])


def join(two, out, groups, heads):
    rows, width = out.shape
    step = rows * width // (groups * width + LANES)
    end = groups * step
    lane, other = (iota((LANES, LANES), axis) for axis in range(2))
    slots = heads * SLOTS
    hot = jnp.logical_and(lane % heads == other % heads, lane // slots == other // slots)
    hot = jnp.logical_and(hot, lane // heads % SLOTS < PIECES).astype(F32).astype(BF16)
    stats = [read_stats(two[i, end:, :]) for i in range(2)]
    for group in range(groups):
        part = slice(group * step, (group + 1) * step)
        scores = [expand_stats(x, heads, group) for x in stats]
        out[part, :] = merge([two[i, part, :].astype(F32) for i in range(2)], scores).astype(BF16)
    left, right = (dot(x, hot) for x in stats)
    top = jnp.maximum(left, right)
    lse = top + jnp.log(jnp.exp(left - top) + jnp.exp(right - top))
    write_stats(out, end, pack_stats(lse, heads))


def join_kernel(groups, skip, odd_ref, *rest):
    count = len(rest) // 2
    two = rest[-1]
    heads = two.shape[2] // HD
    odd_z = lax.axis_index("seq") & 1
    for e in range(count):
        two[odd_z] = rest[e][...]
        two[1 - odd_z] = odd_ref[skip + e]
        join(two, rest[count + e], groups, heads)


def merge_kernel(dys, seqs, groups, w_ref, *rest):
    half = seqs // 2
    ins, (out_ref, pays, two, cross) = rest[:-4], rest[-4:]
    all_rows, width = cross.shape
    heads = width // HD
    pairs = lax.axis_size("req") // CORES
    yed = lax.axis_index("req") // CORES
    zed = lax.axis_index("seq")
    odd_z = zed & 1
    for dy in dys:
        base = lax.rem(yed + dy, pairs) * half
        if dy:
            zero, one, *far = ins[: half + 1]
            two[odd_z] = zero[...]
            two[1 - odd_z] = one[...]
            join(two, pays.at[base + zed // 2], groups, heads)
        else:
            zero, *far = ins[:half]
            pays[base + zed // 2] = zero[...]
        ins = ins[half + 1 if dy else half :]
        for e, ref in enumerate(far, 1):
            pays[base + (zed ^ (2 * e)) // 2] = ref[...]
    total = len(dys) * half
    stats = [read_stats(pays[s, all_rows:, :]) for s in range(total)]
    step = all_rows // groups
    for group in range(groups):
        part = slice(group * step, (group + 1) * step)
        values = [pays[s, part, :].astype(F32) for s in range(total)]
        scores = [expand_stats(stats[s], heads, group) for s in range(total)]
        cross[part, :] = merge(values, scores).astype(BF16)
    out_ref[...] = dot(cross[...], w_ref[...]).astype(BF16)


def gelu(x):
    return 0.5 * x * (1.0 + lax.erf(x * 0.5**0.5))


def ffn_kernel(h_ref, a_ref, b_ref, up_ref, down_ref, h2_ref, out_ref):
    total = h_ref[...].astype(F32) + (a_ref[...].astype(F32) + b_ref[...].astype(F32))
    h2 = normalize(total).astype(BF16)
    h2_ref[...] = h2
    acc = None
    for at in range(0, up_ref.shape[1], CHUNK):
        act = gelu(dot(h2, up_ref[:, at : at + CHUNK])).astype(BF16)
        part = dot(act, down_ref[at : at + CHUNK, :])
        acc = part if acc is None else acc + part
    out_ref[...] = acc.astype(BF16)


def final_kernel(h_ref, a_ref, b_ref, ys_ref, yl_ref):
    total = h_ref[...].astype(F32) + (a_ref[...].astype(F32) + b_ref[...].astype(F32))
    y = normalize(total).astype(BF16)
    short_rows = ys_ref.shape[0] * ys_ref.shape[1]
    ys_ref[...] = y[:short_rows].reshape(ys_ref.shape)
    yl_ref[0] = y[short_rows:]


def call(kernel, name, out, ins, scratch=(), flops=10**8, moved=10**6, grant=16 << 20):
    many = isinstance(out, (tuple, list))
    return pl.pallas_call(
        kernel,
        out_shape=out,
        in_specs=ins,
        out_specs=[VMEM] * len(out) if many else VMEM,
        scratch_shapes=list(scratch),
        name=name,
        cost_estimate=pl.CostEstimate(flops=flops, bytes_accessed=moved, transcendentals=0),
        compiler_params=pltpu.CompilerParams(vmem_limit_bytes=grant),
    )


def in_hbm(x):
    return pltpu.with_memory_space_constraint(x, pltpu.HBM)


def shape(dims, dtype=BF16):
    return jax.ShapeDtypeStruct(dims, dtype)


def local(
    x_short,
    x_long,
    parents,
    long_parents,
    short_len,
    long_len,
    doc_ids,
    long_doc,
    short_kv,
    long_kv,
    enc_kv,
    w_qkv,
    w_out,
    w_cross_q,
    w_cross_out,
    w_up,
    w_down,
):
    requests, rows, model = x_short.shape
    width = w_qkv.shape[2]
    heads = width // HD
    short_rows = requests * rows
    all_rows = short_rows + rows
    seqs = lax.axis_size("seq")
    reqs = lax.axis_size("req")
    tps = lax.axis_size("tp")
    pairs = reqs // CORES
    pay = width + LANES
    span = enc_kv.shape[2]
    both = ("req", "seq")

    def seq_pair(x, k):
        return lax.ppermute(x, "seq", [(i, i ^ k) for i in range(seqs)])

    def yz_move(x, dy, dz):
        perm = []
        for y in range(pairs):
            for c in range(CORES):
                for z in range(seqs):
                    to = ((y + dy) % pairs * CORES + c) * seqs + (z ^ dz)
                    perm.append(((y * CORES + c) * seqs + z, to))
        return lax.ppermute(x, both, perm)

    def tp_swap(x):
        return lax.ppermute(x, "tp", [(i, (i + 1) % tps) for i in range(tps)])

    xs, xl, w_hbm, kv_hbm = map(in_hbm, (x_short, x_long, w_qkv, long_kv))
    queries, inputs, cache, tree = call(
        first_kernel,
        "first",
        (
            shape((all_rows, width)),
            shape((all_rows, model)),
            shape(long_kv.shape[1:]),
            shape((all_rows, rows), F32),
        ),
        [HBM] * 6,
        [
            pltpu.VMEM((model, width), BF16),
            pltpu.VMEM(parents.shape, jnp.int32),
            pltpu.VMEM(long_parents.shape, jnp.int32),
            pltpu.SemaphoreType.DMA((requests + 5,)),
        ],
    )(xs, xl, w_hbm, kv_hbm, in_hbm(parents), in_hbm(long_parents))
    late = (w_qkv, short_kv, w_out, w_cross_q, enc_kv)
    late, queries = lax.optimization_barrier((late, queries))
    w_qkv, short_kv, w_out, w_cross_q, enc_kv = late
    long_pay = call(
        long_kernel, "long", shape((rows, pay)), [VMEM] * 3, flops=8 * 10**9
    )(queries, cache, jnp.broadcast_to(long_len.reshape(1, 1), (1, LANES)))
    got = [seq_pair(long_pay, k) for k in range(1, seqs)]
    other_kv = lax.ppermute(enc_kv, "req", [(i, i ^ 1) for i in range(reqs)])

    attn, draft, stats = call(
        attend_kernel,
        "attend",
        (shape((short_rows, width)), shape((rows, width), F32), shape((rows, LANES))),
        [VMEM] * 5 + [HBM],
        [pltpu.SMEM(short_len.shape, jnp.int32), pltpu.SemaphoreType.DMA((1,))],
        flops=4 * 10**9,
    )(queries, inputs, w_qkv, short_kv, tree, in_hbm(short_len))
    got, attn = lax.optimization_barrier((got, attn))
    partial = call(
        functools.partial(output_kernel, seqs - 1),
        "output",
        shape((all_rows, model)),
        [VMEM] * (4 + seqs),
        [pltpu.VMEM((all_rows, width), BF16), pltpu.VMEM((seqs, rows, pay), BF16)],
    )(attn, draft, stats, w_out, long_pay, *got)

    entries = seqs * requests + 1
    dys = tuple(range(pairs))
    docs, _ = lax.optimization_barrier((doc_ids, partial))
    kvs = call(
        functools.partial(fetch_kernel, seqs, requests, dys),
        "fetch",
        tuple(shape((entries, 2, CORES * span, width)) for _ in dys),
        [SMEM] * 2 + [HBM] * 2,
        [pltpu.SemaphoreType.DMA((pairs, entries, 2))],
        flops=4 * 10**9,
    )(docs, long_doc, in_hbm(enc_kv), other_kv)
    swapped, kvs = lax.optimization_barrier((tp_swap(partial), kvs))
    hidden_one, q_all, q_short = call(
        query_kernel,
        "query",
        (shape((all_rows, model)), shape((all_rows, width)), shape((short_rows, width))),
        [VMEM] * 4,
    )(inputs, partial, swapped, w_cross_q)

    pay_rows = all_rows + rows * LANES // width
    block = shape((pay_rows, width))
    groups = requests + 1
    half = seqs // 2
    odds, evens = list(range(1, seqs, 2)), list(range(2, seqs, 2))

    def near(kv, q, flops):
        return call(
            functools.partial(near_kernel, requests),
            "near",
            (block, shape((rows, width)), shape((rows, LANES), F32)),
            [VMEM] * 2,
            flops=flops,
        )(kv, q)

    def row(stacked, single, kv, long_o, long_stats, q, flops):
        stack = [shape((len(stacked), pay_rows, width))] if stacked else []
        return call(
            functools.partial(row_kernel, requests, stacked, single),
            "row",
            stack + [block] * len(single),
            [VMEM] * 4,
            flops=flops,
        )(kv, long_o, long_stats, q)

    def joined(skip, odd, even, flops):
        return call(
            functools.partial(join_kernel, groups, skip),
            "join",
            [block] * len(even),
            [VMEM] * (1 + len(even)),
            [pltpu.VMEM((2, pay_rows, width), BF16)],
            flops=flops,
        )(odd, *even)

    far_all = [yz_move(q_all, dy, 0) for dy in dys[1:]]
    shifted = [seq_pair(q_short, k) for k in range(1, seqs)]
    zero, *long_part = near(kvs[0], q_all, 10**9)
    shifted, zero = lax.optimization_barrier((shifted, zero))
    own_q = jnp.concatenate(shifted)
    far_q = [yz_move(own_q, dy, 0) for dy in dys[1:]]
    (odd,) = row(odds, [], kvs[0], *long_part, own_q, OWN)
    got = seq_pair(odd, 1)
    even = row([], evens, kvs[0], *long_part, own_q, OWN)
    first, *rest = joined(0, got, [zero, *even], OWN)
    own = [first] + [yz_move(x, 0, e) for e, x in zip(evens, rest)]
    final = []
    for dy in dys[1:]:
        q, even = lax.optimization_barrier((far_all[dy - 1], even))
        zero, *long_part = near(kvs[dy], q, FAR)
        qs, _ = lax.optimization_barrier((far_q[dy - 1], zero))
        odd, one = row(odds[1:], odds[:1], kvs[dy], *long_part, qs, FAR)
        got = seq_pair(odd, 1)
        qs, rest = lax.optimization_barrier((qs, rest))
        even = row([], evens, kvs[dy], *long_part, qs, FAR)
        rest = joined(0, got, even, FAR)
        final += [yz_move(zero, -dy, 0), yz_move(one, -dy, 1)]
        final += [yz_move(x, -dy, e) for e, x in zip(evens, rest)]
    final = own + final
    partial = call(
        functools.partial(merge_kernel, dys, seqs, groups),
        "merge",
        shape((all_rows, model)),
        [VMEM] * (1 + len(final)),
        [
            pltpu.VMEM((pairs * half, pay_rows, width), BF16),
            pltpu.VMEM((2, pay_rows, width), BF16),
            pltpu.VMEM((all_rows, width), BF16),
        ],
    )(w_cross_out, *final)

    hidden_two, partial = call(
        ffn_kernel, "ffn", (shape((all_rows, model)),) * 2, [VMEM] * 5
    )(hidden_one, partial, tp_swap(partial), w_up, w_down)

    return call(
        final_kernel,
        "final",
        (shape((requests, rows, model)), shape((1, rows, model))),
        [VMEM] * 3,
    )(hidden_two, partial, tp_swap(partial))


def solution(mesh):
    in_specs = (
        P(("req", "seq"), None, None),
        P("req", None, None),
        P(("req", "seq"), None),
        P("req", None),
        P(("req", "seq")),
        P("req"),
        P(),
        P(),
        P(("req", "seq"), None, None, "tp"),
        P("req", None, "seq", "tp"),
        P(None, None, ("req", "seq"), "tp"),
        P(None, None, "tp"),
        P("tp", None),
        P(None, "tp"),
        P("tp", None),
        P(None, "tp"),
        P("tp", None),
    )
    out_specs = (P(("req", "seq"), None, None), P("req", None, None))
    return jax.shard_map(local, mesh=mesh, in_specs=in_specs, out_specs=out_specs, check_vma=False)
```

```python
import functools

import jax
import jax.numpy as jnp
from jax import lax
from jax.experimental import pallas as pl
from jax.experimental.pallas import tpu as pltpu
from jax.sharding import PartitionSpec as P

HD = 64
LANES = 128
CORES = 2
PIECES = 3
SLOTS = 4
CHUNK = 2048
OWN = 10**6
FAR = 10**10
MASKED = -1e30
EPS = 1e-05
F32 = jnp.float32
BF16 = jnp.bfloat16
VMEM = pl.BlockSpec(memory_space=pltpu.VMEM)
SMEM = pl.BlockSpec(memory_space=pltpu.SMEM)
HBM = pl.BlockSpec(memory_space=pltpu.HBM)


def iota(shape, axis):
    return lax.broadcasted_iota(jnp.int32, shape, axis)


def dot(a, b):
    return lax.dot_general(a, b, (((1,), (0,)), ((), ())), preferred_element_type=F32)


def dot_t(a, b):
    return lax.dot_general(a, b, (((1,), (1,)), ((), ())), preferred_element_type=F32)


def normalize(v):
    centered = v - jnp.mean(v, axis=-1, keepdims=True)
    return centered * lax.rsqrt(jnp.mean(centered * centered, axis=-1, keepdims=True) + EPS)


def halves(rows, dtype):
    low = (iota((rows, LANES), 1) < HD).astype(F32)
    return low.astype(dtype), (1.0 - low).astype(dtype)


def scores_of(q, k):
    rows, width = q.shape
    low, high = (half * HD ** (-0.5) for half in halves(rows, BF16))
    parts = []
    for at in range(0, width, LANES):
        tile = q[:, at : at + LANES]
        pair = jnp.concatenate([tile * low, tile * high], axis=0)
        parts.append(dot_t(pair, k[:, at : at + LANES]))
    return jnp.concatenate(parts, axis=0)


def sums_of(p):
    return dot(p, jnp.ones((p.shape[1], LANES), BF16))


def values_of(terms, total):
    width = terms[0][1].shape[1]
    rows = total.shape[0] * HD // width
    low = iota((rows, LANES), 1) < HD
    parts = []
    for at in range(0, width, LANES):
        row = at // HD * rows
        mid, end = row + rows, row + 2 * rows
        o = sum(dot(p[row:end], v[:, at : at + LANES]) for p, v in terms)
        o = jnp.where(low, o[:rows], o[rows:])
        parts.append(o / jnp.where(low, total[row:mid], total[mid:end]))
    return jnp.concatenate(parts, axis=1)


def spread(columns, heads):
    rows = columns.shape[0] // heads
    lane = iota((rows, LANES), 1) % heads
    out = jnp.zeros((rows, LANES), F32)
    for h in range(heads):
        out = jnp.where(lane == h, columns[h * rows : (h + 1) * rows], out)
    return out


def pack_stats(lse, heads, group=None):
    place = iota(lse.shape, 1) // heads
    if group is None:
        group, place = 0, place % SLOTS
    high = lse.astype(BF16).astype(F32)
    rest = lse - high
    mid = rest.astype(BF16).astype(F32)
    low = (rest - mid).astype(BF16).astype(F32)
    base = group * SLOTS
    packed = jnp.where(place == base, high, 0.0)
    packed = jnp.where(place == base + 1, mid, packed)
    return jnp.where(place == base + 2, low, packed)


def piece_hot(heads, group, shape, per_head):
    lane = iota(shape, 0)
    place = lane // heads - group * SLOTS
    hot = jnp.logical_and(lane % heads == per_head, place >= 0)
    return jnp.logical_and(hot, place < PIECES).astype(F32).astype(BF16)


def expand_stats(stats, heads, group=0):
    shape = (LANES, heads * HD)
    return dot(stats, piece_hot(heads, group, shape, iota(shape, 1) // HD))


def respread(stats, heads):
    shape = (LANES, LANES)
    return dot(stats, piece_hot(heads, 0, shape, iota(shape, 1) % heads))


def softmax_part(s, v, heads, allowed=None):
    if allowed is not None:
        s = jnp.where(allowed, s, MASKED)
    m = jnp.max(s, axis=-1, keepdims=True)
    p = jnp.exp(s - m)
    if allowed is not None:
        p = jnp.where(allowed, p, 0.0)
    p = p.astype(BF16)
    l = jnp.maximum(sums_of(p), 1e-30)
    return values_of([(p, v)], l), spread(m, heads) + jnp.log(spread(l, heads))


def merge(values, scores):
    top = functools.reduce(jnp.maximum, scores)
    total = acc = None
    for value, score in zip(values, scores):
        w = jnp.exp(score - top)
        total = w if total is None else total + w
        acc = w * value if acc is None else acc + w * value
    return acc / total


def ancestors(parents, rows):
    nodes = parents.shape[1]
    node_j = iota((nodes, nodes), 0)
    node_i = iota((nodes, nodes), 1)
    target = parents + node_i // rows * rows
    hot = jnp.logical_and(target == node_j, node_i % rows > 0).astype(F32)
    closure = (node_i == node_j).astype(F32) + hot
    reach = 1
    while reach < rows:
        b = closure.astype(BF16)
        closure = jnp.minimum(dot(b, b), 1.0)
        reach *= 2
    shape = (nodes, rows)
    place = (iota(shape, 0) % rows == iota(shape, 1)).astype(F32)
    return lax.dot_general(
        closure.astype(BF16),
        place.astype(BF16),
        (((0,), (0,)), ((), ())),
        preferred_element_type=F32,
    )


def first_kernel(
    xs_hbm, xl_hbm, w_hbm, kv_hbm, ps_hbm, lp_hbm, q_ref, x_ref, kv_ref, tree_ref, w, ps, lp, sems
):
    requests, rows, model = xs_hbm.shape
    short_rows = requests * rows
    moves = [(ps_hbm, ps), (lp_hbm, lp)]
    moves += [(xs_hbm.at[j], x_ref.at[pl.ds(j * rows, rows)]) for j in range(requests)]
    moves += [(xl_hbm.at[0], x_ref.at[pl.ds(short_rows, rows)]), (w_hbm.at[0], w)]
    moves += [(kv_hbm.at[0], kv_ref)]
    copies = [pltpu.make_async_copy(a, b, sems.at[i]) for i, (a, b) in enumerate(moves)]
    for copy in copies:
        copy.start()
    for copy in copies[:2]:
        copy.wait()
    parents = [ps[j : j + 1, :] for j in range(requests)] + [lp[...]]
    tree_ref[...] = ancestors(jnp.concatenate(parents, axis=1), rows)
    for copy in copies[2:-1]:
        copy.wait()
    q_ref[...] = dot(x_ref[...], w[...]).astype(BF16)
    copies[-1].wait()


def long_kernel(q_ref, kv_ref, len_ref, pay_ref):
    rows = pay_ref.shape[0]
    width = q_ref.shape[1]
    heads = width // HD
    span = kv_ref.shape[1]
    allowed = iota((1, span), 1) + lax.axis_index("seq") * span < len_ref[:, :1]
    s = scores_of(q_ref[q_ref.shape[0] - rows :, :], kv_ref[0])
    o, lse = softmax_part(s, kv_ref[1], heads, allowed)
    pay_ref[:, :width] = o.astype(BF16)
    pay_ref[:, width:] = pack_stats(lse, heads, 0).astype(BF16)


def short_attend(q, k, v, cache_k, cache_v, allowed, tree, heads):
    allowed_d = jnp.concatenate([tree] * heads, axis=0) > 0.5
    s = jnp.where(allowed, scores_of(q, cache_k), MASKED)
    d = jnp.where(allowed_d, scores_of(q, k), MASKED)
    m = jnp.maximum(jnp.max(s, axis=-1, keepdims=True), jnp.max(d, axis=-1, keepdims=True))
    p = jnp.exp(s - m).astype(BF16)
    pd = jnp.exp(d - m).astype(BF16)
    return values_of([(p, cache_v), (pd, v)], sums_of(p) + sums_of(pd)).astype(BF16)


def attend_kernel(
    q_ref, x_ref, w_ref, skv_ref, tree_ref, sl_hbm, attn_ref, draft_ref, stat_ref, sl, sem
):
    requests = skv_ref.shape[0]
    rows = tree_ref.shape[1]
    copy = pltpu.make_async_copy(sl_hbm, sl, sem.at[0])
    copy.start()
    heads = q_ref.shape[1] // HD
    span = skv_ref.shape[2]
    x = x_ref[...]
    k = dot(x, w_ref[1]).astype(BF16)
    v = dot(x, w_ref[2]).astype(BF16)
    row = requests * rows
    allowed = jnp.concatenate([tree_ref[row:, :]] * heads, axis=0) > 0.5
    s = scores_of(q_ref[row:, :], k[row:])
    o, lse = softmax_part(s, v[row:], heads, allowed)
    draft_ref[...] = o
    stat_ref[...] = pack_stats(lse, heads, 0).astype(BF16)
    copy.wait()
    for j in range(requests):
        part = slice(j * rows, (j + 1) * rows)
        attn_ref[part, :] = short_attend(
            q_ref[part, :], k[part], v[part], skv_ref[j, 0], skv_ref[j, 1],
            iota((1, span), 1) < sl[j], tree_ref[part, :], heads,
        )


def output_kernel(hops, attn_ref, draft_ref, stat_ref, wo_ref, *rest):
    pay_refs, (out_ref, attn, pays) = rest[: hops + 1], rest[hops + 1 :]
    short_rows, width = attn_ref.shape
    heads = width // HD
    zed = lax.axis_index("seq")
    for hop, ref in enumerate(pay_refs):
        pays[zed ^ hop] = ref[...]
    values = [draft_ref[...]] + [pays[z, :, :width].astype(F32) for z in range(hops + 1)]
    scores = [expand_stats(stat_ref[...], heads)] + [
        expand_stats(pays[z, :, width:], heads) for z in range(hops + 1)
    ]
    attn[:short_rows, :] = attn_ref[...]
    attn[short_rows:, :] = merge(values, scores).astype(BF16)
    out_ref[...] = dot(attn[...], wo_ref[...]).astype(BF16)


def query_kernel(x_ref, a_ref, b_ref, w_ref, h_ref, q_ref, qs_ref):
    short_rows = qs_ref.shape[0]
    x = x_ref[...].astype(F32)
    h = normalize(x + (a_ref[...].astype(F32) + b_ref[...].astype(F32))).astype(BF16)
    h_ref[...] = h
    q = dot(h, w_ref[...]).astype(BF16)
    q_ref[...] = q
    qs_ref[...] = q[:short_rows]


def fetch_kernel(seqs, requests, dys, doc_ref, long_ref, own_ref, other_ref, *rest):
    outs, sems = rest[: len(dys)], rest[len(dys)]
    span = own_ref.shape[2]
    short_total = seqs * requests
    zed = lax.axis_index("seq")
    req = lax.axis_index("req")
    pairs = lax.axis_size("req") // CORES
    for at, dy in enumerate(dys):
        group = lax.rem(req // CORES - dy + pairs, pairs) * CORES + lax.rem(req, CORES)
        kv = outs[at]
        copies = []
        for e in range(short_total + 1):
            if e == short_total:
                doc = long_ref[group]
            else:
                place = zed ^ (e // requests)
                doc = doc_ref[(group * seqs + place) * requests + e % requests]
            for half, ref in enumerate((own_ref, other_ref)):
                copies.append(
                    pltpu.make_async_copy(
                        ref.at[:, doc],
                        kv.at[e, :, pl.ds(half * span, span)],
                        sems.at[at, e, half],
                    )
                )
                copies[-1].start()
        if at == 0:
            first = copies
        else:
            first = first + copies
    for copy in first:
        copy.wait()


def document_part(kv_ref, e, q, heads, group):
    o, lse = softmax_part(scores_of(q, kv_ref[e, 0]), kv_ref[e, 1], heads)
    return o.astype(BF16), pack_stats(lse, heads, group)


def fill(pay_ref, parts, long_o, long_stats):
    rows = long_o.shape[0]
    for j, (o, more) in enumerate(parts):
        pay_ref[j * rows : (j + 1) * rows, :] = o
        long_stats = long_stats + more
    end = (len(parts) + 1) * rows
    pay_ref[end - rows : end, :] = long_o
    write_stats(pay_ref, end, long_stats)


def write_stats(pay_ref, row, stats):
    for at in range(0, stats.shape[0], 8):
        lanes = slice(at // 8 * LANES, (at // 8 + 1) * LANES)
        pay_ref[row : row + 8, lanes] = stats[at : at + 8].astype(BF16)


def read_stats(block):
    block = block.astype(F32)
    tiles = [block[:, at : at + LANES] for at in range(0, block.shape[1], LANES)]
    return jnp.concatenate(tiles, axis=0).astype(BF16)


def near_kernel(requests, kv_ref, q_ref, pay_ref, o_ref, stat_ref):
    rows, width = o_ref.shape
    heads = width // HD
    last = q_ref.shape[0] - rows
    o, stats = document_part(kv_ref, kv_ref.shape[0] - 1, q_ref[last:, :], heads, requests)
    o_ref[...] = o
    stat_ref[...] = stats
    parts = [
        document_part(kv_ref, j, q_ref[j * rows : (j + 1) * rows, :], heads, j)
        for j in range(requests)
    ]
    fill(pay_ref, parts, o, stats)


def row_kernel(requests, stacked, single, kv_ref, o_ref, stat_ref, q_ref, *outs):
    ks = stacked + single
    rows, width = o_ref.shape
    heads = width // HD
    targets = [outs[0].at[i] for i in range(len(stacked))]
    targets += outs[1 if stacked else 0 :]
    for k, target in zip(ks, targets):
        parts = []
        for j in range(requests):
            row = ((k - 1) * requests + j) * rows
            q = q_ref[row : row + rows, :]
            parts.append(document_part(kv_ref, k * requests + j, q, heads, j))
        fill(target, parts, o_ref[...], stat_ref[...])


def join(two, out, groups, heads):
    rows, width = out.shape
    step = rows * width // (groups * width + LANES)
    end = groups * step
    lane, other = (iota((LANES, LANES), axis) for axis in range(2))
    slots = heads * SLOTS
    hot = jnp.logical_and(lane % heads == other % heads, lane // slots == other // slots)
    hot = jnp.logical_and(hot, lane // heads % SLOTS < PIECES).astype(F32).astype(BF16)
    stats = [read_stats(two[i, end:, :]) for i in range(2)]
    for group in range(groups):
        part = slice(group * step, (group + 1) * step)
        scores = [expand_stats(x, heads, group) for x in stats]
        out[part, :] = merge([two[i, part, :].astype(F32) for i in range(2)], scores).astype(BF16)
    left, right = (dot(x, hot) for x in stats)
    top = jnp.maximum(left, right)
    lse = top + jnp.log(jnp.exp(left - top) + jnp.exp(right - top))
    write_stats(out, end, pack_stats(lse, heads))


def join_kernel(groups, skip, odd_ref, *rest):
    count = len(rest) // 2
    two = rest[-1]
    heads = two.shape[2] // HD
    odd_z = lax.axis_index("seq") & 1
    for e in range(count):
        two[odd_z] = rest[e][...]
        two[1 - odd_z] = odd_ref[skip + e]
        join(two, rest[count + e], groups, heads)


def merge_kernel(dys, seqs, groups, w_ref, *rest):
    half = seqs // 2
    ins, (out_ref, pays, two, cross) = rest[:-4], rest[-4:]
    all_rows, width = cross.shape
    heads = width // HD
    pairs = lax.axis_size("req") // CORES
    yed = lax.axis_index("req") // CORES
    zed = lax.axis_index("seq")
    odd_z = zed & 1
    for dy in dys:
        base = lax.rem(yed + dy, pairs) * half
        if dy:
            zero, one, *far = ins[: half + 1]
            two[odd_z] = zero[...]
            two[1 - odd_z] = one[...]
            join(two, pays.at[base + zed // 2], groups, heads)
        else:
            zero, *far = ins[:half]
            pays[base + zed // 2] = zero[...]
        ins = ins[half + 1 if dy else half :]
        for e, ref in enumerate(far, 1):
            pays[base + (zed ^ (2 * e)) // 2] = ref[...]
    total = len(dys) * half
    stats = [read_stats(pays[s, all_rows:, :]) for s in range(total)]
    step = all_rows // groups
    for group in range(groups):
        part = slice(group * step, (group + 1) * step)
        values = [pays[s, part, :].astype(F32) for s in range(total)]
        scores = [expand_stats(stats[s], heads, group) for s in range(total)]
        cross[part, :] = merge(values, scores).astype(BF16)
    out_ref[...] = dot(cross[...], w_ref[...]).astype(BF16)


def gelu(x):
    return 0.5 * x * (1.0 + lax.erf(x * 0.5**0.5))


def ffn_kernel(h_ref, a_ref, b_ref, up_ref, down_ref, h2_ref, out_ref):
    total = h_ref[...].astype(F32) + (a_ref[...].astype(F32) + b_ref[...].astype(F32))
    h2 = normalize(total).astype(BF16)
    h2_ref[...] = h2
    acc = None
    for at in range(0, up_ref.shape[1], CHUNK):
        act = gelu(dot(h2, up_ref[:, at : at + CHUNK])).astype(BF16)
        part = dot(act, down_ref[at : at + CHUNK, :])
        acc = part if acc is None else acc + part
    out_ref[...] = acc.astype(BF16)


def final_kernel(h_ref, a_ref, b_ref, ys_ref, yl_ref):
    total = h_ref[...].astype(F32) + (a_ref[...].astype(F32) + b_ref[...].astype(F32))
    y = normalize(total).astype(BF16)
    short_rows = ys_ref.shape[0] * ys_ref.shape[1]
    ys_ref[...] = y[:short_rows].reshape(ys_ref.shape)
    yl_ref[0] = y[short_rows:]


def call(kernel, name, out, ins, scratch=(), flops=10**8, moved=10**6, grant=16 << 20):
    many = isinstance(out, (tuple, list))
    return pl.pallas_call(
        kernel,
        out_shape=out,
        in_specs=ins,
        out_specs=[VMEM] * len(out) if many else VMEM,
        scratch_shapes=list(scratch),
        name=name,
        cost_estimate=pl.CostEstimate(flops=flops, bytes_accessed=moved, transcendentals=0),
        compiler_params=pltpu.CompilerParams(vmem_limit_bytes=grant),
    )


def in_hbm(x):
    return pltpu.with_memory_space_constraint(x, pltpu.HBM)


def shape(dims, dtype=BF16):
    return jax.ShapeDtypeStruct(dims, dtype)


def local(
    x_short,
    x_long,
    parents,
    long_parents,
    short_len,
    long_len,
    doc_ids,
    long_doc,
    short_kv,
    long_kv,
    enc_kv,
    w_qkv,
    w_out,
    w_cross_q,
    w_cross_out,
    w_up,
    w_down,
):
    requests, rows, model = x_short.shape
    width = w_qkv.shape[2]
    heads = width // HD
    short_rows = requests * rows
    all_rows = short_rows + rows
    seqs = lax.axis_size("seq")
    reqs = lax.axis_size("req")
    tps = lax.axis_size("tp")
    pairs = reqs // CORES
    pay = width + LANES
    span = enc_kv.shape[2]
    both = ("req", "seq")

    def seq_pair(x, k):
        return lax.ppermute(x, "seq", [(i, i ^ k) for i in range(seqs)])

    def yz_move(x, dy, dz):
        perm = []
        for y in range(pairs):
            for c in range(CORES):
                for z in range(seqs):
                    to = ((y + dy) % pairs * CORES + c) * seqs + (z ^ dz)
                    perm.append(((y * CORES + c) * seqs + z, to))
        return lax.ppermute(x, both, perm)

    def tp_swap(x):
        return lax.ppermute(x, "tp", [(i, (i + 1) % tps) for i in range(tps)])

    xs, xl, w_hbm, kv_hbm = map(in_hbm, (x_short, x_long, w_qkv, long_kv))
    queries, inputs, cache, tree = call(
        first_kernel,
        "first",
        (
            shape((all_rows, width)),
            shape((all_rows, model)),
            shape(long_kv.shape[1:]),
            shape((all_rows, rows), F32),
        ),
        [HBM] * 6,
        [
            pltpu.VMEM((model, width), BF16),
            pltpu.VMEM(parents.shape, jnp.int32),
            pltpu.VMEM(long_parents.shape, jnp.int32),
            pltpu.SemaphoreType.DMA((requests + 5,)),
        ],
    )(xs, xl, w_hbm, kv_hbm, in_hbm(parents), in_hbm(long_parents))
    late = (w_qkv, short_kv, w_out, w_cross_q, enc_kv)
    late, queries = lax.optimization_barrier((late, queries))
    w_qkv, short_kv, w_out, w_cross_q, enc_kv = late
    long_pay = call(
        long_kernel, "long", shape((rows, pay)), [VMEM] * 3, flops=8 * 10**9
    )(queries, cache, jnp.broadcast_to(long_len.reshape(1, 1), (1, LANES)))
    got = [seq_pair(long_pay, k) for k in range(1, seqs)]
    other_kv = lax.ppermute(enc_kv, "req", [(i, i ^ 1) for i in range(reqs)])

    attn, draft, stats = call(
        attend_kernel,
        "attend",
        (shape((short_rows, width)), shape((rows, width), F32), shape((rows, LANES))),
        [VMEM] * 5 + [HBM],
        [pltpu.SMEM(short_len.shape, jnp.int32), pltpu.SemaphoreType.DMA((1,))],
        flops=4 * 10**9,
    )(queries, inputs, w_qkv, short_kv, tree, in_hbm(short_len))
    got, attn = lax.optimization_barrier((got, attn))
    partial = call(
        functools.partial(output_kernel, seqs - 1),
        "output",
        shape((all_rows, model)),
        [VMEM] * (4 + seqs),
        [pltpu.VMEM((all_rows, width), BF16), pltpu.VMEM((seqs, rows, pay), BF16)],
    )(attn, draft, stats, w_out, long_pay, *got)

    entries = seqs * requests + 1
    dys = tuple(range(pairs))
    docs, _ = lax.optimization_barrier((doc_ids, partial))
    kvs = call(
        functools.partial(fetch_kernel, seqs, requests, dys),
        "fetch",
        tuple(shape((entries, 2, CORES * span, width)) for _ in dys),
        [SMEM] * 2 + [HBM] * 2,
        [pltpu.SemaphoreType.DMA((pairs, entries, 2))],
        flops=4 * 10**9,
    )(docs, long_doc, in_hbm(enc_kv), other_kv)
    swapped, kvs = lax.optimization_barrier((tp_swap(partial), kvs))
    hidden_one, q_all, q_short = call(
        query_kernel,
        "query",
        (shape((all_rows, model)), shape((all_rows, width)), shape((short_rows, width))),
        [VMEM] * 4,
    )(inputs, partial, swapped, w_cross_q)

    pay_rows = all_rows + rows * LANES // width
    block = shape((pay_rows, width))
    groups = requests + 1
    half = seqs // 2
    odds, evens = list(range(1, seqs, 2)), list(range(2, seqs, 2))

    def near(kv, q, flops):
        return call(
            functools.partial(near_kernel, requests),
            "near",
            (block, shape((rows, width)), shape((rows, LANES), F32)),
            [VMEM] * 2,
            flops=flops,
        )(kv, q)

    def row(stacked, single, kv, long_o, long_stats, q, flops):
        stack = [shape((len(stacked), pay_rows, width))] if stacked else []
        return call(
            functools.partial(row_kernel, requests, stacked, single),
            "row",
            stack + [block] * len(single),
            [VMEM] * 4,
            flops=flops,
        )(kv, long_o, long_stats, q)

    def joined(skip, odd, even, flops):
        return call(
            functools.partial(join_kernel, groups, skip),
            "join",
            [block] * len(even),
            [VMEM] * (1 + len(even)),
            [pltpu.VMEM((2, pay_rows, width), BF16)],
            flops=flops,
        )(odd, *even)

    far_all = [yz_move(q_all, dy, 0) for dy in dys[1:]]
    shifted = [seq_pair(q_short, k) for k in range(1, seqs)]
    zero, *long_part = near(kvs[0], q_all, 10**9)
    shifted, zero = lax.optimization_barrier((shifted, zero))
    own_q = jnp.concatenate(shifted)
    far_q = [yz_move(own_q, dy, 0) for dy in dys[1:]]
    (odd,) = row(odds, [], kvs[0], *long_part, own_q, OWN)
    got = seq_pair(odd, 1)
    even = row([], evens, kvs[0], *long_part, own_q, OWN)
    first, *rest = joined(0, got, [zero, *even], OWN)
    own = [first] + [yz_move(x, 0, e) for e, x in zip(evens, rest)]
    final = []
    for dy in dys[1:]:
        q, even = lax.optimization_barrier((far_all[dy - 1], even))
        zero, *long_part = near(kvs[dy], q, FAR)
        qs, _ = lax.optimization_barrier((far_q[dy - 1], zero))
        odd, one = row(odds[1:], odds[:1], kvs[dy], *long_part, qs, FAR)
        got = seq_pair(odd, 1)
        qs, rest = lax.optimization_barrier((qs, rest))
        even = row([], evens, kvs[dy], *long_part, qs, FAR)
        rest = joined(0, got, even, FAR)
        final += [yz_move(zero, -dy, 0), yz_move(one, -dy, 1)]
        final += [yz_move(x, -dy, e) for e, x in zip(evens, rest)]
    final = own + final
    partial = call(
        functools.partial(merge_kernel, dys, seqs, groups),
        "merge",
        shape((all_rows, model)),
        [VMEM] * (1 + len(final)),
        [
            pltpu.VMEM((pairs * half, pay_rows, width), BF16),
            pltpu.VMEM((2, pay_rows, width), BF16),
            pltpu.VMEM((all_rows, width), BF16),
        ],
    )(w_cross_out, *final)

    hidden_two, partial = call(
        ffn_kernel, "ffn", (shape((all_rows, model)),) * 2, [VMEM] * 5
    )(hidden_one, partial, tp_swap(partial), w_up, w_down)

    return call(
        final_kernel,
        "final",
        (shape((requests, rows, model)), shape((1, rows, model))),
        [VMEM] * 3,
    )(hidden_two, partial, tp_swap(partial))


def solution(mesh):
    in_specs = (
        P(("req", "seq"), None, None),
        P("req", None, None),
        P(("req", "seq"), None),
        P("req", None),
        P(("req", "seq")),
        P("req"),
        P(),
        P(),
        P(("req", "seq"), None, None, "tp"),
        P("req", None, "seq", "tp"),
        P(None, None, ("req", "seq"), "tp"),
        P(None, None, "tp"),
        P("tp", None),
        P(None, "tp"),
        P("tp", None),
        P(None, "tp"),
        P("tp", None),
    )
    out_specs = (P(("req", "seq"), None, None), P("req", None, None))
    return jax.shard_map(local, mesh=mesh, in_specs=in_specs, out_specs=out_specs, check_vma=False)
```
